32 devices in a mesh: sx: 4 (over y, x), sy: 2 (over core), op: 4 (over z).
Axes of the slice: x: 2, y: 2, z: 4, core: 2. Of those that a mesh axis runs over, the one named last changes fastest.
Arguments:
- op_real: float32 [4, 2, 6144, 6144], P('sx', 'sy', 'op'), may hold values from -0.0546875 to 0.0546875
- op_imag: float32 [4, 2, 6144, 6144], P('sx', 'sy', 'op'), may hold values from -0.0546875 to 0.0546875
- coef_right: float32 [4, 2, 2, 6144], P('sx', 'sy', None, 'op'), may hold values from -3 to 3
- coef_upper: float32 [4, 2, 2, 6144], P('sx', 'sy', None, 'op'), may hold values from -3 to 3
- sources: float32 [4, 2, 2, 16, 6144], P('sx', 'sy', None, None, 'op'), may hold values from -6 to 6
Outputs:
- traces: float32 [4, 2, 2, 16, 6144], P('sx', 'sy', None, None, 'op')
The draws below stay inside these ranges and needn't reach their ends.
All inputs are finite; a program needn't handle non-finite values.
Results may differ from the reference program's by a relative error of at most 0.0003.
Values sent between devices are 32-bit elements; how exact they have to be, the bound alone decides.
A program may use at most 128 MiB of HBM per device.

```python
import jax
import jax.numpy as jnp
from jax import lax

M = 6144
SRC = 16
NCOL = 4
NROW = 2


def block_levels(own_key, extent, pieces, low, top_value):
    level = 1.0
    for axis_at, blocks in pieces:
        steps = jax.random.uniform(jax.random.fold_in(jax.random.fold_in(own_key, 6), axis_at), (blocks,), jnp.float32, low / len(pieces), top_value / len(pieces))
        level = level * jnp.repeat(jnp.exp(steps), extent[axis_at] // blocks).reshape((-1,) + (1,) * (len(extent) - 1 - axis_at))
    return level


def bell_draw(rng, dims, scale, reach, cuts=(), held_as=jnp.bfloat16):
    values = jax.random.normal(rng, dims, jnp.float32) * scale
    if len(cuts) > 0:
        values = block_levels(rng, dims, cuts, -0.22, 0.18) * values
    return jnp.clip(values, min=-reach, max=reach).astype(held_as)


def setup_inputs(seed: int = 0) -> dict:
    key_list = jax.random.split(jax.random.key(seed), 6)
    return {
        "op_real": bell_draw(key_list[0], (NCOL, NROW, M, M), (2 * M) ** -0.5, 0.0546875, ((0, 4), (1, 2), (2, 4)), jnp.float32),
        "op_imag": bell_draw(key_list[1], (NCOL, NROW, M, M), (2 * M) ** -0.5, 0.0546875, ((0, 4), (1, 2), (2, 4)), jnp.float32),
        "coef_right": bell_draw(key_list[2], (NCOL, NROW, 2, M), 0.5, 3.0, ((0, 4), (1, 2), (3, 4)), jnp.float32),
        "coef_upper": bell_draw(key_list[3], (NCOL, NROW, 2, M), 0.5, 3.0, ((0, 4), (1, 2), (3, 4)), jnp.float32),
        "sources": bell_draw(key_list[4], (NCOL, NROW, 2, SRC, M), 1.0, 6.0, ((0, 4), (1, 2), (4, 4)), jnp.float32),
    }


def contract(left, right):
    return lax.dot_general(left, right, (((1,), (1,)), ((), ())), precision=lax.Precision.HIGHEST, preferred_element_type=jnp.float32)


def complex_scale(coef, field):
    real_part = coef[0][None, :] * field[0] - coef[1][None, :] * field[1]
    imag_part = coef[0][None, :] * field[1] + coef[1][None, :] * field[0]
    return jnp.stack([real_part, imag_part])


def apply_operator(real_mat, imag_mat, field):
    real_part = contract(field[0], real_mat) - contract(field[1], imag_mat)
    imag_part = contract(field[0], imag_mat) + contract(field[1], real_mat)
    return jnp.stack([real_part, imag_part])


def reference(op_real, op_imag, coef_right, coef_upper, sources):
    result = [[None] * NROW for column_at in range(NCOL)]
    for column_at in range(NCOL):
        for row_at in range(NROW):
            incoming = sources[column_at, row_at]
            if column_at > 0:
                incoming = incoming + complex_scale(coef_right[column_at, row_at], result[column_at - 1][row_at])
            if row_at > 0:
                incoming = incoming + complex_scale(coef_upper[column_at, row_at], result[column_at][row_at - 1])
            result[column_at][row_at] = apply_operator(op_real[column_at, row_at], op_imag[column_at, row_at], incoming)
    return jnp.stack([jnp.stack(column_list) for column_list in result])
```

```python
import functools

import jax
import jax.numpy as jnp
from jax import lax
from jax.experimental import pallas as pl
from jax.experimental.pallas import tpu as pltpu
from jax.sharding import PartitionSpec as P

MESH = pl.DeviceIdType.MESH
LANES = 128
LOW_SCALE = 2.0**20
F8 = jnp.float8_e4m3fn
F32 = jnp.float32
BF16 = jnp.bfloat16
NN = (((1,), (0,)), ((), ()))


def kernel(
    ncol, nrow, nop, groups, pieces,
    real_hbm, imag_hbm, right_ref, upper_ref, src_ref, out_ref,
    high, low, stage, gathered, xw, x8, inv, left_buf, below_buf, trace,
    load_sem, gsend, grecv, lsend, lrecv, usend, urecv,
):
    c = lax.axis_index("sx")
    r = lax.axis_index("sy")
    z = lax.axis_index("op")
    first = c + r == 0
    rows, width = real_hbm.shape
    srcs = src_ref.shape[1]
    group_rows = rows // groups
    split = group_rows // LANES
    piece = width // pieces
    blocks = rows // LANES
    ops = (real_hbm, imag_hbm)

    def load(blk, k, p):
        slot = k * pieces + p
        at = pl.multiple_of(blk * LANES, LANES)
        return pltpu.make_async_copy(
            ops[k].at[pl.ds(at, LANES), pl.ds(p * piece, piece)], stage.at[slot], load_sem.at[slot]
        )

    for k in range(2):
        for p in range(pieces):
            load(0, k, p).start()

    barrier = pltpu.get_barrier_semaphore()
    for j in range(1, nop):
        pl.semaphore_signal(
            barrier, inc=1, device_id=(c, r, lax.rem(z + j, nop)), device_id_type=MESH
        )

    def greet(cond, cc, rr):
        @pl.when(cond)
        def _():
            pl.semaphore_signal(barrier, inc=1, device_id=(cc, rr, z), device_id_type=MESH)

    has_left, has_right = c > 0, c < ncol - 1
    has_below, has_above = r > 0, r < nrow - 1
    greet(has_left, c - 1, r)
    greet(has_right, c + 1, r)
    greet(has_below, c, r - 1)
    greet(has_above, c, r + 1)
    near = sum(jnp.where(cond, 1, 0) for cond in (has_left, has_right, has_below, has_above))
    pl.semaphore_wait(barrier, nop - 1 + near)

    def send_right(g):
        return pltpu.make_async_remote_copy(
            trace.at[g], left_buf.at[g], lsend.at[g], lrecv.at[g],
            device_id=(c + 1, r, z), device_id_type=MESH,
        )

    def send_up(g):
        return pltpu.make_async_remote_copy(
            trace.at[g], below_buf.at[g], usend.at[g], urecv.at[g],
            device_id=(c, r + 1, z), device_id_type=MESH,
        )

    def share(g, j):
        peer = lax.rem(z + j, nop)
        return pltpu.make_async_remote_copy(
            gathered.at[z, g], gathered.at[z, g], gsend.at[g, j], grecv.at[g, j],
            device_id=(c, r, peer), device_id_type=MESH,
        )

    def gather():
        for g in range(groups):
            cols = pl.ds(g * group_rows, group_rows)
            gathered[z, g] = src_ref[:, :, cols]

            def add(coef_ref, buf):
                cr = coef_ref[0:1, cols]
                ci = coef_ref[1:2, cols]
                gathered[z, g, 0] += cr * buf[g, 0] - ci * buf[g, 1]
                gathered[z, g, 1] += cr * buf[g, 1] + ci * buf[g, 0]

            @pl.when(has_left)
            def _():
                send_right(g).wait_recv()
                add(right_ref, left_buf)

            @pl.when(has_below)
            def _():
                send_up(g).wait_recv()
                add(upper_ref, below_buf)

            for j in range(1, nop):
                share(g, j).start()
        for g in range(groups):
            for j in range(1, nop):
                share(g, j).wait()

        def largest(step, top):
            zz, g = step // groups, lax.rem(step, groups)
            both = jnp.maximum(jnp.abs(gathered[zz, g, 0]), jnp.abs(gathered[zz, g, 1]))
            return jnp.maximum(top, jnp.max(both, axis=1, keepdims=True))

        top = lax.fori_loop(0, nop * groups, largest, jnp.zeros((srcs, 1), F32))
        top = jnp.maximum(top, 1e-30)
        inv[...] = jnp.broadcast_to(top * (1.0 / (256.0 * LOW_SCALE)), inv.shape)
        scale = 256.0 / top

        @pl.loop(0, nop * groups)
        def _(step):
            zz, g = step // groups, lax.rem(step, groups)
            for h in range(split):
                lanes = slice(h * LANES, (h + 1) * LANES)
                at = step * split + h
                for k in range(2):
                    value = gathered[zz, g, k, :, lanes]
                    top_part = value.astype(BF16)
                    xw[at, k * srcs:(k + 1) * srcs, :] = top_part
                    xw[at, (2 + k) * srcs:(3 + k) * srcs, :] = (
                        value - top_part.astype(F32)
                    ).astype(BF16)
                both = jnp.concatenate(
                    [gathered[zz, g, 0, :, lanes] * scale, gathered[zz, g, 1, :, lanes] * scale],
                    axis=0,
                )
                x8[at] = both.astype(F8)

    def convert(blk):
        for k in range(2):
            for p in range(pieces):
                load(blk, k, p).wait()
                value = stage[k * pieces + p].T
                top_part = value.astype(BF16)
                cols = slice(p * piece, (p + 1) * piece)
                high[k, blk, cols, :] = top_part
                low[k, blk, cols, :] = ((value - top_part.astype(F32)) * LOW_SCALE).astype(F8)

                @pl.when(blk + 1 < blocks)
                def _():
                    load(blk + 1, k, p).start()

    def side(ref):
        return jnp.concatenate([ref[j] for j in range(width // LANES)], axis=1)

    def weights(ref, k, g):
        return jnp.concatenate([ref[k, g * split + h] for h in range(split)], axis=1)

    def multiply(g):
        parts = []
        wide, narrow = side(xw), side(x8)
        factor = jnp.concatenate([inv[:, :1], inv[:, :1]], axis=0)
        for k in range(2):
            big = lax.dot_general(wide, weights(high, k, g), NN, preferred_element_type=F32)
            small = lax.dot_general(narrow, weights(low, k, g), NN, preferred_element_type=F32)
            parts.append(big[:2 * srcs] + (big[2 * srcs:] + small * factor))
        trace[g, 0] = parts[0][:srcs] - parts[1][srcs:]
        trace[g, 1] = parts[1][:srcs] + parts[0][srcs:]

    def publish(g):
        @pl.when(has_right)
        def _():
            send_right(g).start()

        @pl.when(has_above)
        def _():
            send_up(g).start()

        out_ref[:, :, pl.ds(pl.multiple_of(g * group_rows, LANES), group_rows)] = trace[g]

    @pl.when(first)
    def _():
        gather()

    @pl.loop(0, groups)
    def _(g):
        @pl.loop(0, split)
        def _(h):
            convert(g * split + h)

        @pl.when(first)
        def _():
            multiply(g)
            publish(g)

    @pl.when(jnp.logical_not(first))
    def _():
        gather()

        @pl.loop(0, groups)
        def _(g):
            multiply(g)
            publish(g)

    for g in range(groups):
        @pl.when(has_right)
        def _():
            send_right(g).wait_send()

        @pl.when(has_above)
        def _():
            send_up(g).wait_send()


def solution(mesh):
    ncol, nrow, nop = (mesh.shape[a] for a in ("sx", "sy", "op"))

    def shards(op_real, op_imag, coef_right, coef_upper, sources):
        rows, width = op_real.shape[2:]
        srcs = sources.shape[3]
        groups = rows // 256 if rows % 256 == 0 else rows // 128
        group_rows = rows // groups
        pieces = 2 if width % 256 == 0 else 1
        vmem = pl.BlockSpec(memory_space=pltpu.VMEM)
        hbm = pl.BlockSpec(memory_space=pl.ANY)
        dma = pltpu.SemaphoreType.DMA
        out = pl.pallas_call(
            functools.partial(kernel, ncol, nrow, nop, groups, pieces),
            out_shape=jax.ShapeDtypeStruct((2, srcs, rows), F32),
            in_specs=[hbm, hbm, vmem, vmem, vmem],
            out_specs=vmem,
            scratch_shapes=[
                pltpu.VMEM((2, rows // LANES, width, LANES), BF16),
                pltpu.VMEM((2, rows // LANES, width, LANES), F8),
                pltpu.VMEM((2 * pieces, LANES, width // pieces), F32),
                pltpu.VMEM((nop, groups, 2, srcs, group_rows), F32),
                pltpu.VMEM((width // LANES, 4 * srcs, LANES), BF16),
                pltpu.VMEM((width // LANES, 2 * srcs, LANES), F8),
                pltpu.VMEM((srcs, 128), F32),
                pltpu.VMEM((groups, 2, srcs, group_rows), F32),
                pltpu.VMEM((groups, 2, srcs, group_rows), F32),
                pltpu.VMEM((groups, 2, srcs, group_rows), F32),
                dma((2 * pieces,)),
                dma((groups, nop)),
                dma((groups, nop)),
                dma((groups,)),
                dma((groups,)),
                dma((groups,)),
                dma((groups,)),
            ],
            compiler_params=pltpu.CompilerParams(
                collective_id=0, has_side_effects=True, vmem_limit_bytes=67043328
            ),
        )(op_real[0, 0], op_imag[0, 0], coef_right[0, 0], coef_upper[0, 0], sources[0, 0])
        return out[None, None]

    return jax.shard_map(
        shards,
        mesh=mesh,
        in_specs=(
            P("sx", "sy", "op", None),
            P("sx", "sy", "op", None),
            P("sx", "sy", None, "op"),
            P("sx", "sy", None, "op"),
            P("sx", "sy", None, None, "op"),
        ),
        out_specs=P("sx", "sy", None, None, "op"),
        check_vma=False,
    )
```

```python
import functools

import jax
import jax.numpy as jnp
from jax import lax
from jax.experimental import pallas as pl
from jax.experimental.pallas import tpu as pltpu
from jax.sharding import PartitionSpec as P

MESH = pl.DeviceIdType.MESH
LANES = 128
STREAM_SLOTS = 6
AHEAD = 2
PIECES = 3
LOAD_SLOTS = 5
LOW_SCALE = 2.0**20
F8 = jnp.float8_e4m3fn
F32 = jnp.float32
BF16 = jnp.bfloat16
NN = (((1,), (0,)), ((), ()))
NT = (((1,), (1,)), ((), ()))


def kernel(
    ncol, nrow, nop, groups, pieces,
    real_hbm, imag_hbm, right_ref, upper_ref, src_ref, out_ref,
    gathered, xw, x8, inv, left_buf, below_buf, trace,
    load_sem, gsend, grecv, lsend, lrecv, usend, urecv,
):
    c = lax.axis_index("sx")
    r = lax.axis_index("sy")
    z = lax.axis_index("op")
    first = c + r == 0
    rows, width = real_hbm.shape
    srcs = src_ref.shape[1]
    group_rows = rows // groups
    split = group_rows // LANES
    piece = width // pieces
    blocks = rows // LANES
    ops = (real_hbm, imag_hbm)
    has_left, has_right = c > 0, c < ncol - 1
    has_below, has_above = r > 0, r < nrow - 1

    def meet():
        barrier = pltpu.get_barrier_semaphore()
        for j in range(1, nop):
            pl.semaphore_signal(
                barrier, inc=1, device_id=(c, r, lax.rem(z + j, nop)), device_id_type=MESH
            )

        def greet(cond, cc, rr):
            @pl.when(cond)
            def _():
                pl.semaphore_signal(barrier, inc=1, device_id=(cc, rr, z), device_id_type=MESH)

        greet(has_left, c - 1, r)
        greet(has_right, c + 1, r)
        greet(has_below, c, r - 1)
        greet(has_above, c, r + 1)
        near = sum(jnp.where(cond, 1, 0) for cond in (has_left, has_right, has_below, has_above))
        pl.semaphore_wait(barrier, nop - 1 + near)

    def send_right(g):
        return pltpu.make_async_remote_copy(
            trace.at[g], left_buf.at[g], lsend.at[g], lrecv.at[g],
            device_id=(c + 1, r, z), device_id_type=MESH,
        )

    def send_up(g):
        return pltpu.make_async_remote_copy(
            trace.at[g], below_buf.at[g], usend.at[g], urecv.at[g],
            device_id=(c, r + 1, z), device_id_type=MESH,
        )

    def share(g, j):
        peer = lax.rem(z + j, nop)
        return pltpu.make_async_remote_copy(
            gathered.at[z, g], gathered.at[z, g], gsend.at[g, j], grecv.at[g, j],
            device_id=(c, r, peer), device_id_type=MESH,
        )

    def span(g):
        return pl.ds(pl.multiple_of(g * group_rows, LANES), group_rows)

    def publish(g):
        @pl.when(has_right)
        def _():
            send_right(g).start()

        @pl.when(has_above)
        def _():
            send_up(g).start()

        out_ref[:, :, span(g)] = trace[g]

    def arrive(g):
        cols = span(g)
        gathered[z, g] = src_ref[:, :, cols]

        def add(coef_ref, buf):
            cr = coef_ref[0:1, cols]
            ci = coef_ref[1:2, cols]
            gathered[z, g, 0] += cr * buf[g, 0] - ci * buf[g, 1]
            gathered[z, g, 1] += cr * buf[g, 1] + ci * buf[g, 0]

        @pl.when(has_left)
        def _():
            send_right(g).wait_recv()
            add(right_ref, left_buf)

        @pl.when(has_below)
        def _():
            send_up(g).wait_recv()
            add(upper_ref, below_buf)

        for j in range(1, nop):
            share(g, j).start()

    def prepare(steps, slot):
        most = None
        for zz, g in steps:
            both = jnp.maximum(jnp.abs(gathered[zz, g, 0]), jnp.abs(gathered[zz, g, 1]))
            most = both if most is None else jnp.maximum(most, both)
        top = jnp.maximum(jnp.max(most, axis=1, keepdims=True), 1e-30)
        scale = 256.0 / top
        back = top * (1.0 / (256.0 * LOW_SCALE))
        inv[slot] = jnp.broadcast_to(jnp.concatenate([back, back], axis=0), (2 * srcs, LANES))
        for zz, g in steps:
            for h in range(split):
                lanes = slice(h * LANES, (h + 1) * LANES)
                at = (zz * groups + g) * split + h
                for k in range(2):
                    value = gathered[zz, g, k, :, lanes]
                    top_part = value.astype(BF16)
                    xw[at, k * srcs:(k + 1) * srcs, :] = top_part
                    xw[at, (2 + k) * srcs:(3 + k) * srcs, :] = (
                        value - top_part.astype(F32)
                    ).astype(BF16)
                x8[at] = jnp.concatenate(
                    [gathered[zz, g, 0, :, lanes] * scale, gathered[zz, g, 1, :, lanes] * scale],
                    axis=0,
                ).astype(F8)

    def side(ref, steps):
        return jnp.concatenate(
            [ref[(zz * groups + g) * split + h] for zz, g in steps for h in range(split)], axis=1
        )

    def merge(big, small, slot):
        return big[:2 * srcs] + (big[2 * srcs:] + small * inv[slot][:, :1])

    def stream(stage):
        slots = stage.shape[0]
        seg = rows
        paired = (groups - 1) // 2 * 2
        early = nop * paired
        half = nop // 2
        chunks = early + 2 * half * (groups - paired)

        def units(i):
            k = lax.rem(i, 2)
            a, b = i // 2, (i - early) // 2
            in_pairs = i < early
            first_m = jnp.where(in_pairs, 2 * lax.rem(a, paired // 2), paired + b // half)
            first_j = jnp.where(in_pairs, a // (paired // 2), 2 * lax.rem(b, half))
            second_m = jnp.where(in_pairs, first_m + 1, first_m)
            second_j = jnp.where(in_pairs, first_j, first_j + 1)
            return k, ((first_m, first_j), (second_m, second_j))

        def owner(j):
            return lax.rem(z - j + nop, nop)

        def load(i, u, op_k):
            _, pair = units(i)
            m, j = pair[u]
            slot = lax.rem(i, slots)
            return pltpu.make_async_copy(
                ops[op_k].at[
                    pl.ds(pl.multiple_of(m * group_rows, LANES), group_rows),
                    pl.ds(pl.multiple_of(owner(j) * seg, LANES), seg),
                ],
                stage.at[slot, u], load_sem.at[slot, u],
            )

        def fetch(i, op_k):
            for u in range(2):
                load(i, u, op_k).start()

        for i in range(slots):
            fetch(i, i % 2)
        meet()
        for g in range(groups):
            gathered[z, g] = src_ref[:, :, g * group_rows:(g + 1) * group_rows]
        for g in range(groups):
            for j in range(1, nop):
                share(g, j).start()
        trace[...] = jnp.zeros_like(trace)

        def chunk(i, op_k):
            _, pair = units(i)
            slot = lax.rem(i, slots)
            for u in range(2):
                load(i, u, op_k).wait()
            for u in range(2):
                m, j = pair[u]
                steps = [(owner(j), g) for g in range(groups)]
                value = stage[slot, u]
                top_part = value.astype(BF16)
                rest = ((value - top_part.astype(F32)) * LOW_SCALE).astype(F8)
                big = lax.dot_general(side(xw, steps), top_part, NT, preferred_element_type=F32)
                small = lax.dot_general(side(x8, steps), rest, NT, preferred_element_type=F32)
                part = merge(big, small, j)
                if op_k == 0:
                    trace[m, 0] += part[:srcs]
                    trace[m, 1] += part[srcs:]
                else:
                    trace[m, 0] -= part[srcs:]
                    trace[m, 1] += part[:srcs]

            @pl.when(i + slots < chunks)
            def _():
                fetch(i + slots, op_k)

        @pl.loop(0, nop)
        def _(j):
            @pl.when(j > 0)
            def _():
                for g in range(groups):
                    share(g, j).wait()

            prepare([(owner(j), g) for g in range(groups)], j)

            @pl.loop(0, paired // 2)
            def _(a):
                for op_k in range(2):
                    chunk(2 * (j * (paired // 2) + a) + op_k, op_k)

        @pl.loop(0, paired)
        def _(m):
            publish(m)

        @pl.loop(0, groups - paired)
        def _(n):
            @pl.loop(0, half)
            def _(b):
                for op_k in range(2):
                    chunk(early + 2 * (n * half + b) + op_k, op_k)

            publish(paired + n)

    def resident(stage, high, low):
        slots = stage.shape[0]
        per = 2 * pieces
        chunks = per * blocks

        def load(i, n):
            k, p = n // pieces, n % pieces
            at = pl.multiple_of((i // per) * LANES, LANES)
            slot = lax.rem(i, slots)
            return pltpu.make_async_copy(
                ops[k].at[pl.ds(at, LANES), pl.ds(p * piece, piece)],
                stage.at[slot], load_sem.at[slot, 0],
            )

        for i in range(slots):
            load(i, i % per).start()
        meet()

        @pl.loop(0, blocks)
        def _(blk):
            for n in range(per):
                i = blk * per + n
                load(i, n).wait()
                value = stage[lax.rem(i, slots)].T
                top_part = value.astype(BF16)
                k, p = n // pieces, n % pieces
                cols = slice(p * piece, (p + 1) * piece)
                high[k, blk, cols, :] = top_part
                low[k, blk, cols, :] = ((value - top_part.astype(F32)) * LOW_SCALE).astype(F8)

                @pl.when(i + slots < chunks)
                def _():
                    load(i + slots, (n + slots) % per).start()

        trace[...] = jnp.zeros_like(trace)

        def weights(ref, k, m, g):
            tiles = []
            for zz in range(nop):
                at = pl.ds(pl.multiple_of(zz * rows + g * group_rows, LANES), group_rows)
                tiles.append(jnp.concatenate(
                    [ref[k, m * split + h, at, :] for h in range(split)], axis=1
                ))
            return jnp.concatenate(tiles, axis=0)

        def multiply(m, g):
            steps = [(zz, g) for zz in range(nop)]
            wide, narrow = side(xw, steps), side(x8, steps)
            parts = []
            for k in range(2):
                big = lax.dot_general(wide, weights(high, k, m, g), NN, preferred_element_type=F32)
                small = lax.dot_general(narrow, weights(low, k, m, g), NN, preferred_element_type=F32)
                parts.append(merge(big, small, g))
            trace[m, 0] += parts[0][:srcs] - parts[1][srcs:]
            trace[m, 1] += parts[1][:srcs] + parts[0][srcs:]

        together = 2 if groups % 2 == 0 else 1
        for g in range(min(AHEAD, groups)):
            arrive(g)

        @pl.loop(0, groups)
        def _(g):
            @pl.when(g + AHEAD < groups)
            def _():
                arrive(g + AHEAD)

            for j in range(1, nop):
                share(g, j).wait()
            prepare([(zz, g) for zz in range(nop)], g)

            @pl.loop(0, groups // together)
            def _(a):
                for n in range(together):
                    multiply(a * together + n, g)

                @pl.when(g == groups - 1)
                def _():
                    for n in range(together):
                        publish(a * together + n)

    @pl.when(first)
    def _():
        pl.run_scoped(stream, pltpu.VMEM((STREAM_SLOTS, 2, group_rows, rows), F32))

    @pl.when(jnp.logical_not(first))
    def _():
        pl.run_scoped(
            resident,
            pltpu.VMEM((LOAD_SLOTS, LANES, piece), F32),
            pltpu.VMEM((2, blocks, width, LANES), BF16),
            pltpu.VMEM((2, blocks, width, LANES), F8),
        )

    for g in range(groups):
        @pl.when(has_right)
        def _():
            send_right(g).wait_send()

        @pl.when(has_above)
        def _():
            send_up(g).wait_send()


def solution(mesh):
    ncol, nrow, nop = (mesh.shape[a] for a in ("sx", "sy", "op"))

    def shards(op_real, op_imag, coef_right, coef_upper, sources):
        rows, width = op_real.shape[2:]
        srcs = sources.shape[3]
        groups = rows // 256 if rows % 256 == 0 else rows // 128
        group_rows = rows // groups
        pieces = PIECES if width % (PIECES * LANES) == 0 else 1
        vmem = pl.BlockSpec(memory_space=pltpu.VMEM)
        hbm = pl.BlockSpec(memory_space=pl.ANY)
        dma = pltpu.SemaphoreType.DMA
        out = pl.pallas_call(
            functools.partial(kernel, ncol, nrow, nop, groups, pieces),
            out_shape=jax.ShapeDtypeStruct((2, srcs, rows), F32),
            in_specs=[hbm, hbm, vmem, vmem, vmem],
            out_specs=vmem,
            scratch_shapes=[
                pltpu.VMEM((nop, groups, 2, srcs, group_rows), F32),
                pltpu.VMEM((width // LANES, 4 * srcs, LANES), BF16),
                pltpu.VMEM((width // LANES, 2 * srcs, LANES), F8),
                pltpu.VMEM((max(groups, nop), 2 * srcs, LANES), F32),
                pltpu.VMEM((groups, 2, srcs, group_rows), F32),
                pltpu.VMEM((groups, 2, srcs, group_rows), F32),
                pltpu.VMEM((groups, 2, srcs, group_rows), F32),
                dma((max(STREAM_SLOTS, LOAD_SLOTS), 2)),
                dma((groups, nop)),
                dma((groups, nop)),
                dma((groups,)),
                dma((groups,)),
                dma((groups,)),
                dma((groups,)),
            ],
            compiler_params=pltpu.CompilerParams(
                collective_id=0, has_side_effects=True, vmem_limit_bytes=67043328
            ),
        )(op_real[0, 0], op_imag[0, 0], coef_right[0, 0], coef_upper[0, 0], sources[0, 0])
        return out[None, None]

    return jax.shard_map(
        shards,
        mesh=mesh,
        in_specs=(
            P("sx", "sy", "op", None),
            P("sx", "sy", "op", None),
            P("sx", "sy", None, "op"),
            P("sx", "sy", None, "op"),
            P("sx", "sy", None, None, "op"),
        ),
        out_specs=P("sx", "sy", None, None, "op"),
        check_vma=False,
    )
```

```python
import functools

import jax
import jax.numpy as jnp
from jax import lax
from jax.experimental import pallas as pl
from jax.experimental.pallas import tpu as pltpu
from jax.sharding import PartitionSpec as P

MESH = pl.DeviceIdType.MESH
LANES = 128
STREAM_SLOTS = 6
AHEAD = 2
PIECES = 3
LOAD_SLOTS = 5
LOW_SCALE = 2.0**20
F8 = jnp.float8_e4m3fn
F32 = jnp.float32
BF16 = jnp.bfloat16
NN = (((1,), (0,)), ((), ()))
NT = (((1,), (1,)), ((), ()))


def kernel(
    ncol, nrow, nop, groups, pieces,
    real_hbm, imag_hbm, right_ref, upper_ref, src_ref, out_ref,
    gathered, xw, x8, inv, mix, trace, mate_right, mate_upper, mate_src,
    load_sem, hsend, msend, grecv, lsend, lrecv, psend, precv,
):
    c = lax.axis_index("sx")
    r = lax.axis_index("sy")
    z = lax.axis_index("op")
    first = c + r == 0
    rows, width = real_hbm.shape
    srcs = src_ref.shape[1]
    group_rows = rows // groups
    split = group_rows // LANES
    piece = width // pieces
    blocks = rows // LANES
    ops = (real_hbm, imag_hbm)
    has_left, has_right = c > 0, c < ncol - 1
    has_below, has_above = r > 0, r < nrow - 1

    mate = 1 - r
    order = [nop // 2] if nop % 2 == 0 else []
    for j in range((nop - 1) // 2, 0, -1):
        order = [j, nop - j] + order

    def swap():
        pairs = ((right_ref, mate_right), (upper_ref, mate_upper), (src_ref, mate_src))
        return [
            pltpu.make_async_remote_copy(
                mine, theirs, psend.at[n], precv.at[n],
                device_id=(c, mate, z), device_id_type=MESH,
            )
            for n, (mine, theirs) in enumerate(pairs)
        ]

    def meet():
        barrier = pltpu.get_barrier_semaphore()

        def greet(cc, rr, zz):
            pl.semaphore_signal(barrier, inc=1, device_id=(cc, rr, zz), device_id_type=MESH)

        greet(c, mate, z)
        for j in range(1, nop):
            peer = lax.rem(z + j, nop)
            greet(c, r, peer)
            greet(c, mate, peer)

        @pl.when(has_left)
        def _():
            greet(c - 1, mate, z)

        @pl.when(has_right)
        def _():
            greet(c + 1, mate, z)

        near = jnp.where(has_left, 1, 0) + jnp.where(has_right, 1, 0)
        pl.semaphore_wait(barrier, 2 * nop - 1 + near)
        for copy in swap():
            copy.start()

    def send_right(g):
        return pltpu.make_async_remote_copy(
            trace.at[g], mix.at[g], lsend.at[g], lrecv.at[g],
            device_id=(c + 1, mate, z), device_id_type=MESH,
        )

    def lent(g, j):
        return pltpu.make_async_remote_copy(
            mix.at[g], gathered.at[z, g], hsend.at[g, j], grecv.at[g, j],
            device_id=(c, mate, lax.rem(z + j, nop)), device_id_type=MESH,
        )

    def passed(g, j):
        return pltpu.make_async_remote_copy(
            gathered.at[z, g], gathered.at[z, g], msend.at[g, j], grecv.at[g, j],
            device_id=(c, r, lax.rem(z + j, nop)), device_id_type=MESH,
        )

    def each(g, j, by_mate, act):
        if 2 * j == nop:
            @pl.when(lax.rem(g, 2) == (0 if by_mate else 1))
            def _():
                act(g, j)
        elif (2 * j < nop) == by_mate:
            act(g, j)

    def start_lent(g, j):
        lent(g, j).start()

    def start_passed(g, j):
        passed(g, j).start()

    def span(g):
        return pl.ds(pl.multiple_of(g * group_rows, LANES), group_rows)

    def combine(g, with_left, with_own):
        cols = span(g)

        def term(coef_ref, buf, k):
            cr = coef_ref[0:1, cols]
            ci = coef_ref[1:2, cols]
            if k == 0:
                return cr * buf[g, 0] - ci * buf[g, 1]
            return cr * buf[g, 1] + ci * buf[g, 0]

        values = [mate_src[k, :, cols] for k in range(2)]
        if with_left:
            send_right(g).wait_recv()
            values = [values[k] + term(mate_right, mix, k) for k in range(2)]
        if with_own:
            values = [values[k] + term(mate_upper, trace, k) for k in range(2)]
        for k in range(2):
            mix[g, k] = values[k]
        lent(g, 0).start()
        for j in order:
            each(g, j, True, start_lent)

    def publish(g):
        @pl.when(has_right)
        def _():
            send_right(g).start()

        out_ref[:, :, span(g)] = trace[g]

    def take(g):
        passed(g, 0).wait_recv()
        for j in order:
            each(g, j, False, start_passed)

    def prepare(steps, slot):
        most = None
        for zz, g in steps:
            both = jnp.maximum(jnp.abs(gathered[zz, g, 0]), jnp.abs(gathered[zz, g, 1]))
            most = both if most is None else jnp.maximum(most, both)
        top = jnp.maximum(jnp.max(most, axis=1, keepdims=True), 1e-30)
        scale = 256.0 / top
        back = top * (1.0 / (256.0 * LOW_SCALE))
        inv[slot] = jnp.broadcast_to(jnp.concatenate([back, back], axis=0), (2 * srcs, LANES))
        for zz, g in steps:
            for h in range(split):
                lanes = slice(h * LANES, (h + 1) * LANES)
                at = (zz * groups + g) * split + h
                for k in range(2):
                    value = gathered[zz, g, k, :, lanes]
                    top_part = value.astype(BF16)
                    xw[at, k * srcs:(k + 1) * srcs, :] = top_part
                    xw[at, (2 + k) * srcs:(3 + k) * srcs, :] = (
                        value - top_part.astype(F32)
                    ).astype(BF16)
                x8[at] = jnp.concatenate(
                    [gathered[zz, g, 0, :, lanes] * scale, gathered[zz, g, 1, :, lanes] * scale],
                    axis=0,
                ).astype(F8)

    def side(ref, steps):
        return jnp.concatenate(
            [ref[(zz * groups + g) * split + h] for zz, g in steps for h in range(split)], axis=1
        )

    def merge(big, small, slot):
        return big[:2 * srcs] + (big[2 * srcs:] + small * inv[slot][:, :1])

    def stream(stage):
        slots = stage.shape[0]
        seg = rows
        paired = (groups - 1) // 2 * 2
        early = nop * paired
        half = nop // 2
        chunks = early + 2 * half * (groups - paired)

        def units(i):
            k = lax.rem(i, 2)
            a, b = i // 2, (i - early) // 2
            in_pairs = i < early
            first_m = jnp.where(in_pairs, 2 * lax.rem(a, paired // 2), paired + b // half)
            first_j = jnp.where(in_pairs, a // (paired // 2), 2 * lax.rem(b, half))
            second_m = jnp.where(in_pairs, first_m + 1, first_m)
            second_j = jnp.where(in_pairs, first_j, first_j + 1)
            return k, ((first_m, first_j), (second_m, second_j))

        def hop(n):
            return jnp.where(lax.rem(n, 2) == 1, (n + 1) // 2, lax.rem(nop - n // 2, nop))

        def owner(n):
            return lax.rem(z - hop(n) + nop, nop)

        def load(i, u, op_k):
            _, pair = units(i)
            m, j = pair[u]
            slot = lax.rem(i, slots)
            return pltpu.make_async_copy(
                ops[op_k].at[
                    pl.ds(pl.multiple_of(m * group_rows, LANES), group_rows),
                    pl.ds(pl.multiple_of(owner(j) * seg, LANES), seg),
                ],
                stage.at[slot, u], load_sem.at[slot, u],
            )

        def fetch(i, op_k):
            for u in range(2):
                load(i, u, op_k).start()

        for i in range(slots):
            fetch(i, i % 2)
        meet()
        for g in range(groups):
            gathered[z, g] = src_ref[:, :, g * group_rows:(g + 1) * group_rows]
        for j in order:
            for g in range(groups):
                each(g, j, False, start_passed)
        trace[...] = jnp.zeros_like(trace)

        def chunk(i, op_k):
            _, pair = units(i)
            slot = lax.rem(i, slots)
            for u in range(2):
                load(i, u, op_k).wait()
            for u in range(2):
                m, j = pair[u]
                steps = [(owner(j), g) for g in range(groups)]
                value = stage[slot, u]
                top_part = value.astype(BF16)
                rest = ((value - top_part.astype(F32)) * LOW_SCALE).astype(F8)
                big = lax.dot_general(side(xw, steps), top_part, NT, preferred_element_type=F32)
                small = lax.dot_general(side(x8, steps), rest, NT, preferred_element_type=F32)
                part = merge(big, small, j)
                if op_k == 0:
                    trace[m, 0] += part[:srcs]
                    trace[m, 1] += part[srcs:]
                else:
                    trace[m, 0] -= part[srcs:]
                    trace[m, 1] += part[:srcs]

            @pl.when(i + slots < chunks)
            def _():
                fetch(i + slots, op_k)

        @pl.loop(0, nop)
        def _(j):
            @pl.when(j > 0)
            def _():
                for g in range(groups):
                    passed(g, hop(j)).wait_recv()

            prepare([(owner(j), g) for g in range(groups)], j)

            @pl.loop(0, paired // 2)
            def _(a):
                for op_k in range(2):
                    chunk(2 * (j * (paired // 2) + a) + op_k, op_k)

        for copy in swap():
            copy.wait_recv()

        def give(m):
            publish(m)
            combine(m, False, True)

        @pl.loop(0, paired)
        def _(m):
            give(m)

        @pl.loop(0, groups - paired)
        def _(n):
            @pl.loop(0, half)
            def _(b):
                for op_k in range(2):
                    chunk(early + 2 * (n * half + b) + op_k, op_k)

            give(paired + n)

    def resident(stage, high, low):
        slots = stage.shape[0]
        per = 2 * pieces
        chunks = per * blocks

        def load(i, n):
            k, p = n // pieces, n % pieces
            at = pl.multiple_of((i // per) * LANES, LANES)
            slot = lax.rem(i, slots)
            return pltpu.make_async_copy(
                ops[k].at[pl.ds(at, LANES), pl.ds(p * piece, piece)],
                stage.at[slot], load_sem.at[slot, 0],
            )

        for i in range(slots):
            load(i, i % per).start()
        meet()
        for copy in swap():
            copy.wait_recv()

        @pl.when(c == 0)
        def _():
            for g in range(groups):
                mix[g] = mate_src[:, :, g * group_rows:(g + 1) * group_rows]
            for j in order:
                for g in range(groups):
                    each(g, j, True, start_lent)

        @pl.loop(0, blocks)
        def _(blk):
            for n in range(per):
                i = blk * per + n
                load(i, n).wait()
                value = stage[lax.rem(i, slots)].T
                top_part = value.astype(BF16)
                k, p = n // pieces, n % pieces
                cols = slice(p * piece, (p + 1) * piece)
                high[k, blk, cols, :] = top_part
                low[k, blk, cols, :] = ((value - top_part.astype(F32)) * LOW_SCALE).astype(F8)

                @pl.when(i + slots < chunks)
                def _():
                    load(i + slots, (n + slots) % per).start()

        trace[...] = jnp.zeros_like(trace)

        def weights(ref, k, m, g):
            tiles = []
            for zz in range(nop):
                at = pl.ds(pl.multiple_of(zz * rows + g * group_rows, LANES), group_rows)
                tiles.append(jnp.concatenate(
                    [ref[k, m * split + h, at, :] for h in range(split)], axis=1
                ))
            return jnp.concatenate(tiles, axis=0)

        def multiply(m, g):
            steps = [(zz, g) for zz in range(nop)]
            wide, narrow = side(xw, steps), side(x8, steps)
            parts = []
            for k in range(2):
                big = lax.dot_general(wide, weights(high, k, m, g), NN, preferred_element_type=F32)
                small = lax.dot_general(narrow, weights(low, k, m, g), NN, preferred_element_type=F32)
                parts.append(merge(big, small, g))
            trace[m, 0] += parts[0][:srcs] - parts[1][srcs:]
            trace[m, 1] += parts[1][:srcs] + parts[0][srcs:]

        @pl.when(jnp.logical_and(r == 1, c > 0))
        def _():
            @pl.loop(0, groups)
            def _(g):
                combine(g, True, False)

        together = 3 if groups % 3 == 0 else 1
        ahead = jnp.where(c + r == 1, 1, AHEAD)

        @pl.loop(0, ahead)
        def _(g):
            take(g)

        @pl.loop(0, groups)
        def _(g):
            @pl.when(g + ahead < groups)
            def _():
                take(g + ahead)

            for j in range(1, nop):
                passed(g, j).wait_recv()
            prepare([(zz, g) for zz in range(nop)], g)

            @pl.loop(0, groups // together)
            def _(a):
                for n in range(together):
                    multiply(a * together + n, g)

                @pl.when(g == groups - 1)
                def _():
                    for n in range(together):
                        publish(a * together + n)

        @pl.when(r == 0)
        def _():
            @pl.loop(0, groups)
            def _(g):
                combine(g, True, True)

    @pl.when(first)
    def _():
        pl.run_scoped(stream, pltpu.VMEM((STREAM_SLOTS, 2, group_rows, rows), F32))

    @pl.when(jnp.logical_not(first))
    def _():
        pl.run_scoped(
            resident,
            pltpu.VMEM((LOAD_SLOTS, LANES, piece), F32),
            pltpu.VMEM((2, blocks, width, LANES), BF16),
            pltpu.VMEM((2, blocks, width, LANES), F8),
        )

    for copy in swap():
        copy.wait_send()

    def sent_lent(g, j):
        lent(g, j).wait_send()

    def sent_passed(g, j):
        passed(g, j).wait_send()

    @pl.loop(0, groups)
    def _(g):
        @pl.when(has_right)
        def _():
            send_right(g).wait_send()

        @pl.when(c + mate > 0)
        def _():
            lent(g, 0).wait_send()

        for j in order:
            each(g, j, True, sent_lent)
            each(g, j, False, sent_passed)


def solution(mesh):
    ncol, nrow, nop = (mesh.shape[a] for a in ("sx", "sy", "op"))

    def shards(op_real, op_imag, coef_right, coef_upper, sources):
        rows, width = op_real.shape[2:]
        srcs = sources.shape[3]
        groups = rows // 256 if rows % 256 == 0 else rows // 128
        group_rows = rows // groups
        pieces = PIECES if width % (PIECES * LANES) == 0 else 1
        vmem = pl.BlockSpec(memory_space=pltpu.VMEM)
        hbm = pl.BlockSpec(memory_space=pl.ANY)
        dma = pltpu.SemaphoreType.DMA
        out = pl.pallas_call(
            functools.partial(kernel, ncol, nrow, nop, groups, pieces),
            out_shape=jax.ShapeDtypeStruct((2, srcs, rows), F32),
            in_specs=[hbm, hbm, vmem, vmem, vmem],
            out_specs=vmem,
            scratch_shapes=[
                pltpu.VMEM((nop, groups, 2, srcs, group_rows), F32),
                pltpu.VMEM((width // LANES, 4 * srcs, LANES), BF16),
                pltpu.VMEM((width // LANES, 2 * srcs, LANES), F8),
                pltpu.VMEM((max(groups, nop), 2 * srcs, LANES), F32),
                pltpu.VMEM((groups, 2, srcs, group_rows), F32),
                pltpu.VMEM((groups, 2, srcs, group_rows), F32),
                pltpu.VMEM((2, rows), F32),
                pltpu.VMEM((2, rows), F32),
                pltpu.VMEM((2, srcs, rows), F32),
                dma((max(STREAM_SLOTS, LOAD_SLOTS), 2)),
                dma((groups, nop)),
                dma((groups, nop)),
                dma((groups, nop)),
                dma((groups,)),
                dma((groups,)),
                dma((3,)),
                dma((3,)),
            ],
            compiler_params=pltpu.CompilerParams(
                collective_id=0, has_side_effects=True, vmem_limit_bytes=67043328
            ),
        )(op_real[0, 0], op_imag[0, 0], coef_right[0, 0], coef_upper[0, 0], sources[0, 0])
        return out[None, None]

    return jax.shard_map(
        shards,
        mesh=mesh,
        in_specs=(
            P("sx", "sy", "op", None),
            P("sx", "sy", "op", None),
            P("sx", "sy", None, "op"),
            P("sx", "sy", None, "op"),
            P("sx", "sy", None, None, "op"),
        ),
        out_specs=P("sx", "sy", None, None, "op"),
        check_vma=False,
    )
```

```python
import functools

import jax
import jax.numpy as jnp
from jax import lax
from jax.experimental import pallas as pl
from jax.experimental.pallas import tpu as pltpu
from jax.sharding import PartitionSpec as P

MESH = pl.DeviceIdType.MESH
LANES = 128
STREAM_SLOTS = 6
LAST = 3
PIECES = 3
LOAD_SLOTS = 4
LOW_SCALE = 2.0**20
F8 = jnp.float8_e4m3fn
F32 = jnp.float32
BF16 = jnp.bfloat16
NN = (((1,), (0,)), ((), ()))
NT = (((1,), (1,)), ((), ()))


def kernel(
    ncol, nrow, nop, groups, pieces,
    real_hbm, imag_hbm, right_ref, upper_ref, src_ref, out_ref,
    src_all, right_all, upper_all, left_all, below_all, trace, inv,
    load_sem, isend, irecv, lsend, lrecv, usend, bsend, brecv,
):
    c = lax.axis_index("sx")
    r = lax.axis_index("sy")
    z = lax.axis_index("op")
    first = c + r == 0
    rows, width = real_hbm.shape
    srcs = src_ref.shape[1]
    group_rows = rows // groups
    split = group_rows // LANES
    piece = width // pieces
    blocks = rows // LANES
    ops = (real_hbm, imag_hbm)
    has_left, has_right = c > 0, c < ncol - 1
    has_below, has_above = r > 0, r < nrow - 1

    mate = 1 - r
    lower = r == 0

    def peer(j):
        return lax.rem(z + j, nop)

    def meet():
        barrier = pltpu.get_barrier_semaphore()

        def greet(cc, rr, zz):
            pl.semaphore_signal(barrier, inc=1, device_id=(cc, rr, zz), device_id_type=MESH)

        for j in range(nop):
            greet(c, mate, peer(j))
        for j in range(1, nop):
            greet(c, r, peer(j))
        for there, step in ((has_right, 1), (has_left, -1)):
            @pl.when(there)
            def _():
                for j in range(nop):
                    greet(c + step, r, peer(j))

        near = jnp.where(has_left, nop, 0) + jnp.where(has_right, nop, 0)
        pl.semaphore_wait(barrier, 2 * nop - 1 + near)
        src_all[z] = src_ref[...]
        right_all[z] = right_ref[...]
        upper_all[z] = upper_ref[...]

    def spread():
        for n in (2, 0, 1):
            for j in range(1, nop):
                fill(n, j).start()

    def fill(n, j):
        mine, whole = ((right_ref, right_all), (upper_ref, upper_all), (src_ref, src_all))[n]
        return pltpu.make_async_remote_copy(
            mine, whole.at[z], isend.at[n, j], irecv.at[n, j],
            device_id=(c, r, peer(j)), device_id_type=MESH,
        )

    def to_right(g, j):
        return pltpu.make_async_remote_copy(
            trace.at[g], left_all.at[z, g], lsend.at[g, j], lrecv.at[g, j],
            device_id=(c + 1, r, peer(j)), device_id_type=MESH,
        )

    def to_upper(g, j):
        return pltpu.make_async_remote_copy(
            trace.at[g], below_all.at[z, g], usend.at[g, j], brecv.at[g, j],
            device_id=(c, mate, peer(j)), device_id_type=MESH,
        )

    def along(g, j):
        return pltpu.make_async_remote_copy(
            left_all.at[z, g], left_all.at[z, g], bsend.at[g, j], lrecv.at[g, j],
            device_id=(c, r, peer(j)), device_id_type=MESH,
        )

    def span(g):
        return pl.ds(pl.multiple_of(g * group_rows, LANES), group_rows)

    def publish(g):
        @pl.when(has_right)
        def _():
            to_right(g, 0).start()

            @pl.when(has_below)
            def _():
                for j in range(1, nop):
                    to_right(g, j).start()

        @pl.when(lower)
        def _():
            for j in range(nop):
                to_upper(g, j).start()

        out_ref[:, :, span(g)] = trace[g]

    def take():
        @pl.when(jnp.logical_and(lower, has_left))
        def _():
            @pl.loop(0, groups)
            def _(g):
                to_right(g, 0).wait_recv()
                for j in range(1, nop):
                    along(g, j).start()

    def arrived(g):
        @pl.when(has_left)
        def _():
            for j in range(1, nop):
                to_right(g, j).wait_recv()

        @pl.when(has_below)
        def _():
            @pl.when(has_left)
            def _():
                to_right(g, 0).wait_recv()

            for j in range(nop):
                to_upper(g, j).wait_recv()

    def source(zz, g, h):
        cols = pl.ds(pl.multiple_of(g * group_rows + h * LANES, LANES), LANES)
        return [src_all[zz, k, :, cols] for k in range(2)]

    def incoming(zz, g, h):
        cols = pl.ds(pl.multiple_of(g * group_rows + h * LANES, LANES), LANES)
        lanes = slice(h * LANES, (h + 1) * LANES)
        value = source(zz, g, h)
        for coef, field in ((right_all, left_all), (upper_all, below_all)):
            cr, ci = coef[zz, 0:1, cols], coef[zz, 1:2, cols]
            fr, fi = field[zz, g, 0, :, lanes], field[zz, g, 1, :, lanes]
            value = [value[0] + (cr * fr - ci * fi), value[1] + (cr * fi + ci * fr)]
        return value

    def prepare(get, steps, slot, xw, x8, base):
        pairs = [get(zz, g, h) for zz, g in steps for h in range(split)]
        most = None
        for pair in pairs:
            both = jnp.maximum(jnp.abs(pair[0]), jnp.abs(pair[1]))
            most = both if most is None else jnp.maximum(most, both)
        top = jnp.maximum(jnp.max(most, axis=1, keepdims=True), 1e-30)
        scale = 256.0 / top
        back = top * (1.0 / (256.0 * LOW_SCALE))
        inv[slot] = jnp.broadcast_to(jnp.concatenate([back, back], axis=0), (2 * srcs, LANES))
        for n, pair in enumerate(pairs):
            for k in range(2):
                top_part = pair[k].astype(BF16)
                xw[base + n, k * srcs:(k + 1) * srcs, :] = top_part
                xw[base + n, (2 + k) * srcs:(3 + k) * srcs, :] = (
                    pair[k] - top_part.astype(F32)
                ).astype(BF16)
            x8[base + n] = jnp.concatenate([pair[0] * scale, pair[1] * scale], axis=0).astype(F8)

    def side(ref, base, count):
        return jnp.concatenate([ref[base + n] for n in range(count)], axis=1)

    def merge(big, small, slot):
        return big[:2 * srcs] + (big[2 * srcs:] + small * inv[slot][:, :1])

    def stream(stage, xw, x8):
        slots = stage.shape[0]
        seg = rows
        paired = (groups - 1) // 2 * 2
        early = nop * paired
        half = nop // 2
        chunks = early + 2 * half * (groups - paired)

        def units(i):
            k = lax.rem(i, 2)
            a, b = i // 2, (i - early) // 2
            in_pairs = i < early
            first_m = jnp.where(in_pairs, 2 * lax.rem(a, paired // 2), paired + b // half)
            first_j = jnp.where(in_pairs, a // (paired // 2), 2 * lax.rem(b, half))
            second_m = jnp.where(in_pairs, first_m + 1, first_m)
            second_j = jnp.where(in_pairs, first_j, first_j + 1)
            return k, ((first_m, first_j), (second_m, second_j))

        def hop(n):
            return jnp.where(lax.rem(n, 2) == 1, (n + 1) // 2, lax.rem(nop - n // 2, nop))

        def owner(n):
            return lax.rem(z - hop(n) + nop, nop)

        def load(i, u, op_k):
            _, pair = units(i)
            m, j = pair[u]
            slot = lax.rem(i, slots)
            return pltpu.make_async_copy(
                ops[op_k].at[
                    pl.ds(pl.multiple_of(m * group_rows, LANES), group_rows),
                    pl.ds(pl.multiple_of(owner(j) * seg, LANES), seg),
                ],
                stage.at[slot, u], load_sem.at[slot, u],
            )

        def fetch(i, op_k):
            for u in range(2):
                load(i, u, op_k).start()

        for i in range(slots):
            fetch(i, i % 2)
        meet()
        spread()
        trace[...] = jnp.zeros_like(trace)

        def chunk(i, op_k):
            _, pair = units(i)
            slot = lax.rem(i, slots)
            for u in range(2):
                load(i, u, op_k).wait()
            for u in range(2):
                m, j = pair[u]
                base = owner(j) * (groups * split)
                value = stage[slot, u]
                top_part = value.astype(BF16)
                rest = ((value - top_part.astype(F32)) * LOW_SCALE).astype(F8)
                big = lax.dot_general(side(xw, base, groups * split), top_part, NT, preferred_element_type=F32)
                small = lax.dot_general(side(x8, base, groups * split), rest, NT, preferred_element_type=F32)
                part = merge(big, small, j)
                if op_k == 0:
                    trace[m, 0] += part[:srcs]
                    trace[m, 1] += part[srcs:]
                else:
                    trace[m, 0] -= part[srcs:]
                    trace[m, 1] += part[:srcs]

            @pl.when(i + slots < chunks)
            def _():
                fetch(i + slots, op_k)

        @pl.loop(0, nop)
        def _(j):
            @pl.when(j > 0)
            def _():
                for n in range(3):
                    fill(n, hop(j)).wait_recv()

            steps = [(owner(j), g) for g in range(groups)]
            prepare(source, steps, j, xw, x8, owner(j) * (groups * split))

            @pl.loop(0, paired // 2)
            def _(a):
                for op_k in range(2):
                    chunk(2 * (j * (paired // 2) + a) + op_k, op_k)

        @pl.loop(0, paired)
        def _(m):
            publish(m)

        @pl.loop(0, groups - paired)
        def _(n):
            @pl.loop(0, half)
            def _(b):
                for op_k in range(2):
                    chunk(early + 2 * (n * half + b) + op_k, op_k)

            publish(paired + n)

    def resident(stage, high, low, xw, x8):
        slots = stage.shape[0]
        per = 2 * pieces
        chunks = per * blocks

        def load(i, n):
            k, p = n // pieces, n % pieces
            at = pl.multiple_of((i // per) * LANES, LANES)
            slot = lax.rem(i, slots)
            return pltpu.make_async_copy(
                ops[k].at[pl.ds(at, LANES), pl.ds(p * piece, piece)],
                stage.at[slot], load_sem.at[slot, 0],
            )

        for i in range(slots):
            load(i, i % per).start()
        meet()

        @pl.when(lower)
        def _():
            spread()


        @pl.when(jnp.logical_not(has_left))
        def _():
            left_all[...] = jnp.zeros_like(left_all)

        @pl.when(jnp.logical_not(has_below))
        def _():
            below_all[...] = jnp.zeros_like(below_all)

        @pl.loop(0, blocks)
        def _(blk):
            @pl.when(jnp.logical_and(has_below, blk == blocks // 2 - 1))
            def _():
                spread()

            for n in range(per):
                i = blk * per + n
                load(i, n).wait()
                value = stage[lax.rem(i, slots)].T
                top_part = value.astype(BF16)
                k, p = n // pieces, n % pieces
                cols = slice(p * piece, (p + 1) * piece)
                high[k, blk, cols, :] = top_part
                low[k, blk, cols, :] = ((value - top_part.astype(F32)) * LOW_SCALE).astype(F8)

                @pl.when(i + slots < chunks)
                def _():
                    load(i + slots, (n + slots) % per).start()

        trace[...] = jnp.zeros_like(trace)

        def weights(ref, k, m, g):
            tiles = []
            for zz in range(nop):
                at = pl.ds(pl.multiple_of(zz * rows + g * group_rows, LANES), group_rows)
                tiles.append(jnp.concatenate(
                    [ref[k, m * split + h, at, :] for h in range(split)], axis=1
                ))
            return jnp.concatenate(tiles, axis=0)

        count = nop * split

        def multiply(m, pairs):
            wide = jnp.concatenate([side(xw, slot * count, count) for _, slot in pairs], axis=1)
            parts = []
            for k in range(2):
                tall = jnp.concatenate([weights(high, k, m, g) for g, _ in pairs], axis=0)
                part = lax.dot_general(wide, tall, NN, preferred_element_type=F32)
                part = part[:2 * srcs], part[2 * srcs:]
                for g, slot in pairs:
                    small = lax.dot_general(
                        side(x8, slot * count, count), weights(low, k, m, g), NN,
                        preferred_element_type=F32,
                    )
                    part = part[0], part[1] + small * inv[slot][:, :1]
                parts.append(part[0] + part[1])
            trace[m, 0] += parts[0][:srcs] - parts[1][srcs:]
            trace[m, 1] += parts[1][:srcs] + parts[0][srcs:]

        last = min(LAST, groups)
        early = groups - last

        def ready(g, slot):
            arrived(g)
            prepare(incoming, [(zz, g) for zz in range(nop)], slot, xw, x8, slot * count)

        for n in range(3):
            for j in range(1, nop):
                fill(n, j).wait_recv()
        take()

        @pl.loop(0, early)
        def _(g):
            ready(g, 0)
            for m in range(groups):
                multiply(m, [(g, 0)])

        for n in range(last):
            ready(early + n, n)

        @pl.loop(0, groups)
        def _(m):
            multiply(m, [(early + n, n) for n in range(last)])
            publish(m)

    @pl.when(first)
    def _():
        pl.run_scoped(
            stream,
            pltpu.VMEM((STREAM_SLOTS, 2, group_rows, rows), F32),
            pltpu.VMEM((width // LANES, 4 * srcs, LANES), BF16),
            pltpu.VMEM((width // LANES, 2 * srcs, LANES), F8),
        )

    @pl.when(jnp.logical_not(first))
    def _():
        pl.run_scoped(
            resident,
            pltpu.VMEM((LOAD_SLOTS, LANES, piece), F32),
            pltpu.VMEM((2, blocks, width, LANES), BF16),
            pltpu.VMEM((2, blocks, width, LANES), F8),
            pltpu.VMEM((min(LAST, groups) * nop * split, 4 * srcs, LANES), BF16),
            pltpu.VMEM((min(LAST, groups) * nop * split, 2 * srcs, LANES), F8),
        )

    for n in range(3):
        for j in range(1, nop):
            fill(n, j).wait_send()

    @pl.loop(0, groups)
    def _(g):
        @pl.when(has_right)
        def _():
            to_right(g, 0).wait_send()

            @pl.when(has_below)
            def _():
                for j in range(1, nop):
                    to_right(g, j).wait_send()

        @pl.when(lower)
        def _():
            for j in range(nop):
                to_upper(g, j).wait_send()

            @pl.when(has_left)
            def _():
                for j in range(1, nop):
                    along(g, j).wait_send()


def solution(mesh):
    ncol, nrow, nop = (mesh.shape[a] for a in ("sx", "sy", "op"))

    def shards(op_real, op_imag, coef_right, coef_upper, sources):
        rows, width = op_real.shape[2:]
        srcs = sources.shape[3]
        groups = rows // 256 if rows % 256 == 0 else rows // 128
        group_rows = rows // groups
        pieces = PIECES if width % (PIECES * LANES) == 0 else 1
        vmem = pl.BlockSpec(memory_space=pltpu.VMEM)
        hbm = pl.BlockSpec(memory_space=pl.ANY)
        dma = pltpu.SemaphoreType.DMA
        out = pl.pallas_call(
            functools.partial(kernel, ncol, nrow, nop, groups, pieces),
            out_shape=jax.ShapeDtypeStruct((2, srcs, rows), F32),
            in_specs=[hbm, hbm, vmem, vmem, vmem],
            out_specs=vmem,
            scratch_shapes=[
                pltpu.VMEM((nop, 2, srcs, rows), F32),
                pltpu.VMEM((nop, 2, rows), F32),
                pltpu.VMEM((nop, 2, rows), F32),
                pltpu.VMEM((nop, groups, 2, srcs, group_rows), F32),
                pltpu.VMEM((nop, groups, 2, srcs, group_rows), F32),
                pltpu.VMEM((groups, 2, srcs, group_rows), F32),
                pltpu.VMEM((max(LAST, nop), 2 * srcs, LANES), F32),
                dma((max(STREAM_SLOTS, LOAD_SLOTS), 2)),
                dma((3, nop)),
                dma((3, nop)),
                dma((groups, nop)),
                dma((groups, nop)),
                dma((groups, nop)),
                dma((groups, nop)),
                dma((groups, nop)),
            ],
            compiler_params=pltpu.CompilerParams(
                collective_id=0, has_side_effects=True, vmem_limit_bytes=67043328
            ),
        )(op_real[0, 0], op_imag[0, 0], coef_right[0, 0], coef_upper[0, 0], sources[0, 0])
        return out[None, None]

    return jax.shard_map(
        shards,
        mesh=mesh,
        in_specs=(
            P("sx", "sy", "op", None),
            P("sx", "sy", "op", None),
            P("sx", "sy", None, "op"),
            P("sx", "sy", None, "op"),
            P("sx", "sy", None, None, "op"),
        ),
        out_specs=P("sx", "sy", None, None, "op"),
        check_vma=False,
    )
```

```python
import functools

import jax
import jax.numpy as jnp
from jax import lax
from jax.experimental import pallas as pl
from jax.experimental.pallas import tpu as pltpu
from jax.sharding import PartitionSpec as P

MESH = pl.DeviceIdType.MESH
LANES = 128
STREAM_SLOTS = 8
LAST = 3
PIECES = 3
LOAD_SLOTS = 4
LOW_SCALE = 2.0**20
F8 = jnp.float8_e4m3fn
F32 = jnp.float32
BF16 = jnp.bfloat16
NN = (((1,), (0,)), ((), ()))
NT = (((1,), (1,)), ((), ()))


def kernel(
    ncol, nrow, nop, groups, pieces,
    real_hbm, imag_hbm, right_ref, upper_ref, src_ref, out_ref,
    src_all, right_all, upper_all, left_all, below_all, trace, inv,
    load_sem, isend, irecv, lsend, lrecv, usend, bsend, brecv, relay, rrecv,
):
    c = lax.axis_index("sx")
    r = lax.axis_index("sy")
    z = lax.axis_index("op")
    first = c + r == 0
    rows, width = real_hbm.shape
    srcs = src_ref.shape[1]
    group_rows = rows // groups
    split = group_rows // LANES
    piece = width // pieces
    blocks = rows // LANES
    ops = (real_hbm, imag_hbm)
    has_left, has_right = c > 0, c < ncol - 1
    has_below, has_above = r > 0, r < nrow - 1

    mate = 1 - r
    lower = r == 0

    def peer(j):
        return lax.rem(z + j, nop)

    def meet():
        barrier = pltpu.get_barrier_semaphore()

        def greet(cc, rr, zz):
            pl.semaphore_signal(barrier, inc=1, device_id=(cc, rr, zz), device_id_type=MESH)

        for j in range(nop):
            greet(c, mate, peer(j))
        for j in range(1, nop):
            greet(c, r, peer(j))
        for there, step in ((has_right, 1), (has_left, -1)):
            @pl.when(there)
            def _():
                for j in range(nop):
                    greet(c + step, r, peer(j))

        @pl.when(lends)
        def _():
            greet(served, mate, z)

        @pl.when(relays)
        def _():
            greet(served, mate, z)
            for j in range(nop):
                greet(served + 1, mate, peer(j))

        @pl.when(gets)
        def _():
            for j in range(nop):
                greet(lax.rem(c + 1, 4), mate, peer(j))

        near = jnp.where(has_left, nop, 0) + jnp.where(has_right, nop, 0)
        near += jnp.where(lends, 1, 0) + jnp.where(relays, nop + 1, 0) + jnp.where(gets, nop, 0)
        pl.semaphore_wait(barrier, 2 * nop - 1 + near)
        src_all[z] = src_ref[...]
        right_all[z] = right_ref[...]
        upper_all[z] = upper_ref[...]

    def spread():
        for n in (2, 0, 1):
            for j in range(1, nop):
                fill(n, j).start()

    def fill(n, j):
        mine, whole = ((right_ref, right_all), (upper_ref, upper_all), (src_ref, src_all))[n]
        return pltpu.make_async_remote_copy(
            mine, whole.at[z], isend.at[n, j], irecv.at[n, j],
            device_id=(c, r, peer(j)), device_id_type=MESH,
        )

    def to_right(g, j):
        return pltpu.make_async_remote_copy(
            trace.at[g], left_all.at[z, g], lsend.at[g, j], lrecv.at[g, j],
            device_id=(c + 1, r, peer(j)), device_id_type=MESH,
        )

    def to_upper(g, j):
        return pltpu.make_async_remote_copy(
            trace.at[g], below_all.at[z, g], usend.at[g, j], brecv.at[g, j],
            device_id=(c, mate, peer(j)), device_id_type=MESH,
        )

    detour = ncol == 4
    late = (groups - 1) // 2 * 2
    served = lax.rem(c + 2, 4)
    lends = jnp.logical_and(jnp.logical_and(lower, detour), jnp.logical_and(c > 0, has_right))
    relays = jnp.logical_and(
        jnp.logical_and(has_below, detour), jnp.logical_and(served > 0, served < ncol - 1)
    )
    gets = jnp.logical_and(jnp.logical_and(lower, detour), c > 1)

    def straight(g):
        return jnp.logical_or(has_below, jnp.logical_and(c == 0, g < late))

    def lent(g):
        return jnp.logical_and(lends, lax.rem(g, 2) == 0)

    def spreads(g):
        own = jnp.logical_or(c > 1, jnp.logical_and(c == 1, g >= late))
        direct = jnp.logical_and(gets, lax.rem(g, 2) == 0)
        return jnp.logical_and(jnp.logical_and(lower, own), jnp.logical_not(direct))

    def lend(g):
        return pltpu.make_async_remote_copy(
            trace.at[g], relay.at[g], lsend.at[g, 0], rrecv.at[g],
            device_id=(lax.rem(c + 2, 4), mate, z), device_id_type=MESH,
        )

    def pass_on(g, j):
        return pltpu.make_async_remote_copy(
            relay.at[g], left_all.at[z, g], bsend.at[g, j], lrecv.at[g, j],
            device_id=(served + 1, mate, peer(j)), device_id_type=MESH,
        )

    def serve(when):
        @pl.when(jnp.logical_and(relays, when))
        def _():
            @pl.loop(0, (groups + 1) // 2)
            def _(n):
                lend(2 * n).wait_recv()
                for j in range(nop):
                    pass_on(2 * n, j).start()

    def along(g, j):
        return pltpu.make_async_remote_copy(
            left_all.at[z, g], left_all.at[z, g], bsend.at[g, j], lrecv.at[g, j],
            device_id=(c, r, peer(j)), device_id_type=MESH,
        )

    def span(g):
        return pl.ds(pl.multiple_of(g * group_rows, LANES), group_rows)

    def publish(g):
        @pl.when(has_right)
        def _():
            @pl.when(lent(g))
            def _():
                lend(g).start()

            @pl.when(jnp.logical_not(lent(g)))
            def _():
                to_right(g, 0).start()

            @pl.when(straight(g))
            def _():
                for j in range(1, nop):
                    to_right(g, j).start()

        @pl.when(lower)
        def _():
            for j in range(nop):
                to_upper(g, j).start()

        out_ref[:, :, span(g)] = trace[g]

    def take():
        @pl.loop(0, groups)
        def _(g):
            @pl.when(spreads(g))
            def _():
                to_right(g, 0).wait_recv()
                for j in range(1, nop):
                    along(g, j).start()

    def arrived(g):
        @pl.when(has_left)
        def _():
            for j in range(1, nop):
                to_right(g, j).wait_recv()

            @pl.when(jnp.logical_not(spreads(g)))
            def _():
                to_right(g, 0).wait_recv()

        @pl.when(has_below)
        def _():
            for j in range(nop):
                to_upper(g, j).wait_recv()

    def source(zz, g, h):
        cols = pl.ds(pl.multiple_of(g * group_rows + h * LANES, LANES), LANES)
        return [src_all[zz, k, :, cols] for k in range(2)]

    def incoming(zz, g, h):
        cols = pl.ds(pl.multiple_of(g * group_rows + h * LANES, LANES), LANES)
        lanes = slice(h * LANES, (h + 1) * LANES)
        value = source(zz, g, h)
        for coef, field in ((right_all, left_all), (upper_all, below_all)):
            cr, ci = coef[zz, 0:1, cols], coef[zz, 1:2, cols]
            fr, fi = field[zz, g, 0, :, lanes], field[zz, g, 1, :, lanes]
            value = [value[0] + (cr * fr - ci * fi), value[1] + (cr * fi + ci * fr)]
        return value

    def prepare(get, steps, slot, xw, x8, base):
        pairs = [get(zz, g, h) for zz, g in steps for h in range(split)]
        most = None
        for pair in pairs:
            both = jnp.maximum(jnp.abs(pair[0]), jnp.abs(pair[1]))
            most = both if most is None else jnp.maximum(most, both)
        top = jnp.maximum(jnp.max(most, axis=1, keepdims=True), 1e-30)
        scale = 256.0 / top
        back = top * (1.0 / (256.0 * LOW_SCALE))
        inv[slot] = jnp.broadcast_to(jnp.concatenate([back, back], axis=0), (2 * srcs, LANES))
        for n, pair in enumerate(pairs):
            for k in range(2):
                top_part = pair[k].astype(BF16)
                xw[base + n, k * srcs:(k + 1) * srcs, :] = top_part
                xw[base + n, (2 + k) * srcs:(3 + k) * srcs, :] = (
                    pair[k] - top_part.astype(F32)
                ).astype(BF16)
            x8[base + n] = jnp.concatenate([pair[0] * scale, pair[1] * scale], axis=0).astype(F8)

    def side(ref, base, count):
        return jnp.concatenate([ref[base + n] for n in range(count)], axis=1)

    def merge(big, small, slot):
        return big[:2 * srcs] + (big[2 * srcs:] + small * inv[slot][:, :1])

    def stream(stage, xw, x8):
        slots = stage.shape[0]
        seg = rows
        paired = (groups - 1) // 2 * 2
        early = nop * paired
        half = nop // 2
        chunks = early + 2 * half * (groups - paired)

        def units(i):
            k = lax.rem(i, 2)
            a, b = i // 2, (i - early) // 2
            in_pairs = i < early
            first_m = jnp.where(in_pairs, 2 * lax.rem(a, paired // 2), paired + b // half)
            first_j = jnp.where(in_pairs, a // (paired // 2), 2 * lax.rem(b, half))
            second_m = jnp.where(in_pairs, first_m + 1, first_m)
            second_j = jnp.where(in_pairs, first_j, first_j + 1)
            return k, ((first_m, first_j), (second_m, second_j))

        def hop(n):
            return n

        def owner(n):
            return lax.rem(z - hop(n) + nop, nop)

        def load(i, u, op_k):
            _, pair = units(i)
            m, j = pair[u]
            slot = lax.rem(i, slots)
            return pltpu.make_async_copy(
                ops[op_k].at[
                    pl.ds(pl.multiple_of(m * group_rows, LANES), group_rows),
                    pl.ds(pl.multiple_of(owner(j) * seg, LANES), seg),
                ],
                stage.at[slot, u], load_sem.at[slot, u],
            )

        def fetch(i, op_k):
            for u in range(2):
                load(i, u, op_k).start()

        for i in range(slots):
            fetch(i, i % 2)
        meet()
        spread()
        trace[...] = jnp.zeros_like(trace)

        def chunk(i, op_k):
            _, pair = units(i)
            slot = lax.rem(i, slots)
            for u in range(2):
                load(i, u, op_k).wait()
            for u in range(2):
                m, j = pair[u]
                base = owner(j) * (groups * split)
                value = stage[slot, u]
                top_part = value.astype(BF16)
                rest = ((value - top_part.astype(F32)) * LOW_SCALE).astype(F8)
                big = lax.dot_general(side(xw, base, groups * split), top_part, NT, preferred_element_type=F32)
                small = lax.dot_general(side(x8, base, groups * split), rest, NT, preferred_element_type=F32)
                part = merge(big, small, j)
                if op_k == 0:
                    trace[m, 0] += part[:srcs]
                    trace[m, 1] += part[srcs:]
                else:
                    trace[m, 0] -= part[srcs:]
                    trace[m, 1] += part[:srcs]

            @pl.when(i + slots < chunks)
            def _():
                fetch(i + slots, op_k)

        @pl.loop(0, nop)
        def _(j):
            @pl.when(j > 0)
            def _():
                for n in range(3):
                    fill(n, hop(j)).wait_recv()

            steps = [(owner(j), g) for g in range(groups)]
            prepare(source, steps, j, xw, x8, owner(j) * (groups * split))

            @pl.loop(0, paired // 2)
            def _(a):
                for op_k in range(2):
                    chunk(2 * (j * (paired // 2) + a) + op_k, op_k)

        @pl.loop(0, paired)
        def _(m):
            publish(m)

        @pl.loop(0, groups - paired)
        def _(n):
            @pl.loop(0, half)
            def _(b):
                for op_k in range(2):
                    chunk(early + 2 * (n * half + b) + op_k, op_k)

            publish(paired + n)

    def resident(stage, high, low, xw, x8):
        slots = stage.shape[0]
        per = 2 * pieces
        chunks = per * blocks

        def load(i, n):
            k, p = n // pieces, n % pieces
            at = pl.multiple_of((i // per) * LANES, LANES)
            slot = lax.rem(i, slots)
            return pltpu.make_async_copy(
                ops[k].at[pl.ds(at, LANES), pl.ds(p * piece, piece)],
                stage.at[slot], load_sem.at[slot, 0],
            )

        for i in range(slots):
            load(i, i % per).start()
        meet()

        @pl.when(lower)
        def _():
            spread()


        @pl.when(jnp.logical_not(has_left))
        def _():
            left_all[...] = jnp.zeros_like(left_all)

        @pl.when(jnp.logical_not(has_below))
        def _():
            below_all[...] = jnp.zeros_like(below_all)

        @pl.loop(0, blocks)
        def _(blk):
            @pl.when(jnp.logical_and(has_below, blk == blocks // 2 - 1))
            def _():
                spread()

            for n in range(per):
                i = blk * per + n
                load(i, n).wait()
                value = stage[lax.rem(i, slots)].T
                top_part = value.astype(BF16)
                k, p = n // pieces, n % pieces
                cols = slice(p * piece, (p + 1) * piece)
                high[k, blk, cols, :] = top_part
                low[k, blk, cols, :] = ((value - top_part.astype(F32)) * LOW_SCALE).astype(F8)

                @pl.when(i + slots < chunks)
                def _():
                    load(i + slots, (n + slots) % per).start()

        trace[...] = jnp.zeros_like(trace)

        def weights(ref, k, m, g):
            tiles = []
            for zz in range(nop):
                at = pl.ds(pl.multiple_of(zz * rows + g * group_rows, LANES), group_rows)
                tiles.append(jnp.concatenate(
                    [ref[k, m * split + h, at, :] for h in range(split)], axis=1
                ))
            return jnp.concatenate(tiles, axis=0)

        count = nop * split

        def multiply(m, pairs):
            wide = jnp.concatenate([side(xw, slot * count, count) for _, slot in pairs], axis=1)
            parts = []
            for k in range(2):
                tall = jnp.concatenate([weights(high, k, m, g) for g, _ in pairs], axis=0)
                part = lax.dot_general(wide, tall, NN, preferred_element_type=F32)
                part = part[:2 * srcs], part[2 * srcs:]
                for g, slot in pairs:
                    small = lax.dot_general(
                        side(x8, slot * count, count), weights(low, k, m, g), NN,
                        preferred_element_type=F32,
                    )
                    part = part[0], part[1] + small * inv[slot][:, :1]
                parts.append(part[0] + part[1])
            trace[m, 0] += parts[0][:srcs] - parts[1][srcs:]
            trace[m, 1] += parts[1][:srcs] + parts[0][srcs:]

        last = min(LAST, groups)
        early = groups - last

        def ready(g, slot):
            arrived(g)
            prepare(incoming, [(zz, g) for zz in range(nop)], slot, xw, x8, slot * count)

        for n in range(3):
            for j in range(1, nop):
                fill(n, j).wait_recv()
        serve(c > served)
        take()

        @pl.loop(0, early)
        def _(g):
            ready(g, 0)
            for m in range(groups):
                multiply(m, [(g, 0)])

        for n in range(last):
            ready(early + n, n)

        @pl.loop(0, groups)
        def _(m):
            multiply(m, [(early + n, n) for n in range(last)])
            publish(m)

        serve(c < served)

    @pl.when(first)
    def _():
        pl.run_scoped(
            stream,
            pltpu.VMEM((STREAM_SLOTS, 2, group_rows, rows), F32),
            pltpu.VMEM((width // LANES, 4 * srcs, LANES), BF16),
            pltpu.VMEM((width // LANES, 2 * srcs, LANES), F8),
        )

    @pl.when(jnp.logical_not(first))
    def _():
        pl.run_scoped(
            resident,
            pltpu.VMEM((LOAD_SLOTS, LANES, piece), F32),
            pltpu.VMEM((2, blocks, width, LANES), BF16),
            pltpu.VMEM((2, blocks, width, LANES), F8),
            pltpu.VMEM((min(LAST, groups) * nop * split, 4 * srcs, LANES), BF16),
            pltpu.VMEM((min(LAST, groups) * nop * split, 2 * srcs, LANES), F8),
        )

    for n in range(3):
        for j in range(1, nop):
            fill(n, j).wait_send()

    @pl.loop(0, groups)
    def _(g):
        @pl.when(has_right)
        def _():
            to_right(g, 0).wait_send()

            @pl.when(straight(g))
            def _():
                for j in range(1, nop):
                    to_right(g, j).wait_send()

        @pl.when(lower)
        def _():
            for j in range(nop):
                to_upper(g, j).wait_send()

        @pl.when(spreads(g))
        def _():
            for j in range(1, nop):
                along(g, j).wait_send()

        @pl.when(jnp.logical_and(relays, lax.rem(g, 2) == 0))
        def _():
            for j in range(nop):
                pass_on(g, j).wait_send()


def solution(mesh):
    ncol, nrow, nop = (mesh.shape[a] for a in ("sx", "sy", "op"))

    def shards(op_real, op_imag, coef_right, coef_upper, sources):
        rows, width = op_real.shape[2:]
        srcs = sources.shape[3]
        groups = rows // 256 if rows % 256 == 0 else rows // 128
        group_rows = rows // groups
        pieces = PIECES if width % (PIECES * LANES) == 0 else 1
        vmem = pl.BlockSpec(memory_space=pltpu.VMEM)
        hbm = pl.BlockSpec(memory_space=pl.ANY)
        dma = pltpu.SemaphoreType.DMA
        out = pl.pallas_call(
            functools.partial(kernel, ncol, nrow, nop, groups, pieces),
            out_shape=jax.ShapeDtypeStruct((2, srcs, rows), F32),
            in_specs=[hbm, hbm, vmem, vmem, vmem],
            out_specs=vmem,
            scratch_shapes=[
                pltpu.VMEM((nop, 2, srcs, rows), F32),
                pltpu.VMEM((nop, 2, rows), F32),
                pltpu.VMEM((nop, 2, rows), F32),
                pltpu.VMEM((nop, groups, 2, srcs, group_rows), F32),
                pltpu.VMEM((nop, groups, 2, srcs, group_rows), F32),
                pltpu.VMEM((groups, 2, srcs, group_rows), F32),
                pltpu.VMEM((max(LAST, nop), 2 * srcs, LANES), F32),
                dma((max(STREAM_SLOTS, LOAD_SLOTS), 2)),
                dma((3, nop)),
                dma((3, nop)),
                dma((groups, nop)),
                dma((groups, nop)),
                dma((groups, nop)),
                dma((groups, nop)),
                dma((groups, nop)),
                pltpu.VMEM((groups, 2, srcs, group_rows), F32),
                dma((groups,)),
            ],
            compiler_params=pltpu.CompilerParams(
                collective_id=0, has_side_effects=True, vmem_limit_bytes=67043328
            ),
        )(op_real[0, 0], op_imag[0, 0], coef_right[0, 0], coef_upper[0, 0], sources[0, 0])
        return out[None, None]

    return jax.shard_map(
        shards,
        mesh=mesh,
        in_specs=(
            P("sx", "sy", "op", None),
            P("sx", "sy", "op", None),
            P("sx", "sy", None, "op"),
            P("sx", "sy", None, "op"),
            P("sx", "sy", None, None, "op"),
        ),
        out_specs=P("sx", "sy", None, None, "op"),
        check_vma=False,
    )
```

```python
import functools

import jax
import jax.numpy as jnp
from jax import lax
from jax.experimental import pallas as pl
from jax.experimental.pallas import tpu as pltpu
from jax.sharding import PartitionSpec as P

MESH = pl.DeviceIdType.MESH
LANES = 128
STREAM_SLOTS = 8
LAST = 3
PIECES = 3
LOAD_SLOTS = 4
LOW_SCALE = 2.0**20
F8 = jnp.float8_e4m3fn
F32 = jnp.float32
BF16 = jnp.bfloat16
NN = (((1,), (0,)), ((), ()))
NT = (((1,), (1,)), ((), ()))


def kernel(
    ncol, nrow, nop, groups, pieces,
    real_hbm, imag_hbm, right_ref, upper_ref, src_ref, out_ref,
    src_all, right_all, upper_all, left_all, below_all, trace, inv,
    load_sem, isend, irecv, lsend, lrecv, usend, bsend, brecv, relay, rrecv,
):
    c = lax.axis_index("sx")
    r = lax.axis_index("sy")
    z = lax.axis_index("op")
    first = c + r == 0
    rows, width = real_hbm.shape
    srcs = src_ref.shape[1]
    group_rows = rows // groups
    split = group_rows // LANES
    piece = width // pieces
    blocks = rows // LANES
    ops = (real_hbm, imag_hbm)
    has_left, has_right = c > 0, c < ncol - 1
    has_below, has_above = r > 0, r < nrow - 1

    mate = 1 - r
    lower = r == 0

    def peer(j):
        return lax.rem(z + j, nop)

    def meet():
        barrier = pltpu.get_barrier_semaphore()

        def greet(cc, rr, zz):
            pl.semaphore_signal(barrier, inc=1, device_id=(cc, rr, zz), device_id_type=MESH)

        for j in range(nop):
            greet(c, mate, peer(j))
        for j in range(1, nop):
            greet(c, r, peer(j))
        for there, step in ((has_right, 1), (has_left, -1)):
            @pl.when(there)
            def _():
                for j in range(nop):
                    greet(c + step, r, peer(j))

        @pl.when(lends)
        def _():
            greet(served, mate, z)

        @pl.when(relays)
        def _():
            greet(served, mate, z)
            for j in range(nop):
                greet(served + 1, mate, peer(j))

        @pl.when(gets)
        def _():
            for j in range(nop):
                greet(lax.rem(c + 1, 4), mate, peer(j))

        near = jnp.where(has_left, nop, 0) + jnp.where(has_right, nop, 0)
        near += jnp.where(lends, 1, 0) + jnp.where(relays, nop + 1, 0) + jnp.where(gets, nop, 0)
        pl.semaphore_wait(barrier, 2 * nop - 1 + near)
        src_all[z] = src_ref[...]
        right_all[z] = right_ref[...]
        upper_all[z] = upper_ref[...]

    def spread():
        for n in (2, 0, 1):
            for j in range(1, nop):
                fill(n, j).start()

    def fill(n, j):
        mine, whole = ((right_ref, right_all), (upper_ref, upper_all), (src_ref, src_all))[n]
        return pltpu.make_async_remote_copy(
            mine, whole.at[z], isend.at[n, j], irecv.at[n, j],
            device_id=(c, r, peer(j)), device_id_type=MESH,
        )

    def to_right(g, j):
        return pltpu.make_async_remote_copy(
            trace.at[g], left_all.at[z, g], lsend.at[g, j], lrecv.at[g, j],
            device_id=(c + 1, r, peer(j)), device_id_type=MESH,
        )

    def to_upper(g, j):
        return pltpu.make_async_remote_copy(
            trace.at[g], below_all.at[z, g], usend.at[g, j], brecv.at[g, j],
            device_id=(c, mate, peer(j)), device_id_type=MESH,
        )

    detour = ncol == 4
    late = (groups - 1) // 2 * 2
    served = lax.rem(c + 2, 4)
    lends = jnp.logical_and(jnp.logical_and(lower, detour), jnp.logical_and(c > 0, has_right))
    relays = jnp.logical_and(
        jnp.logical_and(has_below, detour), jnp.logical_and(served > 0, served < ncol - 1)
    )
    gets = jnp.logical_and(jnp.logical_and(lower, detour), c > 1)

    def straight(g):
        return jnp.logical_or(has_below, jnp.logical_and(c == 0, g < late))

    def lent(g):
        return jnp.logical_and(lends, lax.rem(g, 2) == 0)

    def spreads(g):
        own = jnp.logical_or(c > 1, jnp.logical_and(c == 1, g >= late))
        direct = jnp.logical_and(gets, lax.rem(g, 2) == 0)
        return jnp.logical_and(jnp.logical_and(lower, own), jnp.logical_not(direct))

    def lend(g):
        return pltpu.make_async_remote_copy(
            trace.at[g], relay.at[g], lsend.at[g, 0], rrecv.at[g],
            device_id=(lax.rem(c + 2, 4), mate, z), device_id_type=MESH,
        )

    def pass_on(g, j):
        return pltpu.make_async_remote_copy(
            relay.at[g], left_all.at[z, g], bsend.at[g, j], lrecv.at[g, j],
            device_id=(served + 1, mate, peer(j)), device_id_type=MESH,
        )

    def serve(when):
        @pl.when(jnp.logical_and(relays, when))
        def _():
            @pl.loop(0, (groups + 1) // 2)
            def _(n):
                lend(2 * n).wait_recv()
                for j in range(nop):
                    pass_on(2 * n, j).start()

    def along(g, j):
        return pltpu.make_async_remote_copy(
            left_all.at[z, g], left_all.at[z, g], bsend.at[g, j], lrecv.at[g, j],
            device_id=(c, r, peer(j)), device_id_type=MESH,
        )

    def span(g):
        return pl.ds(pl.multiple_of(g * group_rows, LANES), group_rows)

    def publish(g):
        @pl.when(has_right)
        def _():
            @pl.when(lent(g))
            def _():
                lend(g).start()

            @pl.when(jnp.logical_not(lent(g)))
            def _():
                to_right(g, 0).start()

            @pl.when(straight(g))
            def _():
                for j in range(1, nop):
                    to_right(g, j).start()

        @pl.when(lower)
        def _():
            for j in range(nop):
                to_upper(g, j).start()

        out_ref[:, :, span(g)] = trace[g]

    def take():
        @pl.loop(0, groups)
        def _(g):
            @pl.when(spreads(g))
            def _():
                to_right(g, 0).wait_recv()
                for j in range(1, nop):
                    along(g, j).start()

    def arrived(g):
        @pl.when(has_left)
        def _():
            for j in range(1, nop):
                to_right(g, j).wait_recv()

            @pl.when(jnp.logical_not(spreads(g)))
            def _():
                to_right(g, 0).wait_recv()

        @pl.when(has_below)
        def _():
            for j in range(nop):
                to_upper(g, j).wait_recv()

    def source(zz, g, h):
        cols = pl.ds(pl.multiple_of(g * group_rows + h * LANES, LANES), LANES)
        return [src_all[zz, k, :, cols] for k in range(2)]

    def incoming(zz, g, h):
        cols = pl.ds(pl.multiple_of(g * group_rows + h * LANES, LANES), LANES)
        lanes = slice(h * LANES, (h + 1) * LANES)
        value = source(zz, g, h)
        for coef, field in ((right_all, left_all), (upper_all, below_all)):
            cr, ci = coef[zz, 0:1, cols], coef[zz, 1:2, cols]
            fr, fi = field[zz, g, 0, :, lanes], field[zz, g, 1, :, lanes]
            value = [value[0] + (cr * fr - ci * fi), value[1] + (cr * fi + ci * fr)]
        return value

    def prepare(get, steps, slot, xw, x8, base):
        pairs = [get(zz, g, h) for zz, g in steps for h in range(split)]
        most = None
        for pair in pairs:
            both = jnp.maximum(jnp.abs(pair[0]), jnp.abs(pair[1]))
            most = both if most is None else jnp.maximum(most, both)
        top = jnp.maximum(jnp.max(most, axis=1, keepdims=True), 1e-30)
        scale = 256.0 / top
        back = top * (1.0 / (256.0 * LOW_SCALE))
        inv[slot] = jnp.broadcast_to(jnp.concatenate([back, back], axis=0), (2 * srcs, LANES))
        for n, pair in enumerate(pairs):
            for k in range(2):
                top_part = pair[k].astype(BF16)
                xw[base + n, k * srcs:(k + 1) * srcs, :] = top_part
                xw[base + n, (2 + k) * srcs:(3 + k) * srcs, :] = (
                    pair[k] - top_part.astype(F32)
                ).astype(BF16)
            x8[base + n] = jnp.concatenate([pair[0] * scale, pair[1] * scale], axis=0).astype(F8)

    def side(ref, base, count):
        return jnp.concatenate([ref[base + n] for n in range(count)], axis=1)

    def merge(big, small, slot):
        return big[:2 * srcs] + (big[2 * srcs:] + small * inv[slot][:, :1])

    def stream(stage, xw, x8):
        slots = stage.shape[0]
        seg = rows
        paired = groups // 2 * 2
        early = nop * paired
        half = nop // 2
        chunks = early + 2 * half * (groups - paired)

        def units(i):
            k = lax.rem(i, 2)
            a, b = i // 2, (i - early) // 2
            in_pairs = i < early
            first_m = jnp.where(in_pairs, 2 * lax.rem(a, paired // 2), paired + b // half)
            first_j = jnp.where(in_pairs, a // (paired // 2), 2 * lax.rem(b, half))
            second_m = jnp.where(in_pairs, first_m + 1, first_m)
            second_j = jnp.where(in_pairs, first_j, first_j + 1)
            return k, ((first_m, first_j), (second_m, second_j))

        def hop(n):
            return n

        def owner(n):
            return lax.rem(z - hop(n) + nop, nop)

        def load(i, u, op_k):
            _, pair = units(i)
            m, j = pair[u]
            slot = lax.rem(i, slots)
            return pltpu.make_async_copy(
                ops[op_k].at[
                    pl.ds(pl.multiple_of(m * group_rows, LANES), group_rows),
                    pl.ds(pl.multiple_of(owner(j) * seg, LANES), seg),
                ],
                stage.at[slot, u], load_sem.at[slot, u],
            )

        def fetch(i, op_k):
            for u in range(2):
                load(i, u, op_k).start()

        for i in range(slots):
            fetch(i, i % 2)
        meet()
        spread()
        trace[...] = jnp.zeros_like(trace)

        def chunk(i, op_k):
            _, pair = units(i)
            slot = lax.rem(i, slots)
            for u in range(2):
                load(i, u, op_k).wait()
            for u in range(2):
                m, j = pair[u]
                base = owner(j) * (groups * split)
                value = stage[slot, u]
                top_part = value.astype(BF16)
                rest = ((value - top_part.astype(F32)) * LOW_SCALE).astype(F8)
                big = lax.dot_general(side(xw, base, groups * split), top_part, NT, preferred_element_type=F32)
                small = lax.dot_general(side(x8, base, groups * split), rest, NT, preferred_element_type=F32)
                part = merge(big, small, j)
                if op_k == 0:
                    trace[m, 0] += part[:srcs]
                    trace[m, 1] += part[srcs:]
                else:
                    trace[m, 0] -= part[srcs:]
                    trace[m, 1] += part[:srcs]

            @pl.when(i + slots < chunks)
            def _():
                fetch(i + slots, op_k)

        @pl.loop(0, nop)
        def _(j):
            @pl.when(j > 0)
            def _():
                for n in range(3):
                    fill(n, hop(j)).wait_recv()

            steps = [(owner(j), g) for g in range(groups)]
            prepare(source, steps, j, xw, x8, owner(j) * (groups * split))

            @pl.loop(0, paired // 2)
            def _(a):
                for op_k in range(2):
                    chunk(2 * (j * (paired // 2) + a) + op_k, op_k)

                @pl.when(j == nop - 1)
                def _():
                    publish(2 * a)
                    publish(2 * a + 1)

        @pl.loop(0, groups - paired)
        def _(n):
            @pl.loop(0, half)
            def _(b):
                for op_k in range(2):
                    chunk(early + 2 * (n * half + b) + op_k, op_k)

            publish(paired + n)

    def resident(stage, high, low, xw, x8):
        slots = stage.shape[0]
        per = 2 * pieces
        chunks = per * blocks

        def load(i, n):
            k, p = n // pieces, n % pieces
            at = pl.multiple_of((i // per) * LANES, LANES)
            slot = lax.rem(i, slots)
            return pltpu.make_async_copy(
                ops[k].at[pl.ds(at, LANES), pl.ds(p * piece, piece)],
                stage.at[slot], load_sem.at[slot, 0],
            )

        for i in range(slots):
            load(i, i % per).start()
        meet()

        @pl.when(lower)
        def _():
            spread()


        @pl.when(jnp.logical_not(has_left))
        def _():
            left_all[...] = jnp.zeros_like(left_all)

        @pl.when(jnp.logical_not(has_below))
        def _():
            below_all[...] = jnp.zeros_like(below_all)

        @pl.loop(0, blocks)
        def _(blk):
            @pl.when(jnp.logical_and(has_below, blk == jnp.where(c == 0, blocks // 3, blocks // 2 - 1)))
            def _():
                spread()

            for n in range(per):
                i = blk * per + n
                load(i, n).wait()
                value = stage[lax.rem(i, slots)].T
                top_part = value.astype(BF16)
                k, p = n // pieces, n % pieces
                cols = slice(p * piece, (p + 1) * piece)
                high[k, blk, cols, :] = top_part
                low[k, blk, cols, :] = ((value - top_part.astype(F32)) * LOW_SCALE).astype(F8)

                @pl.when(i + slots < chunks)
                def _():
                    load(i + slots, (n + slots) % per).start()

        trace[...] = jnp.zeros_like(trace)

        def weights(ref, k, m, g):
            tiles = []
            for zz in range(nop):
                at = pl.ds(pl.multiple_of(zz * rows + g * group_rows, LANES), group_rows)
                tiles.append(jnp.concatenate(
                    [ref[k, m * split + h, at, :] for h in range(split)], axis=1
                ))
            return jnp.concatenate(tiles, axis=0)

        count = nop * split

        def multiply(m, pairs):
            wide = jnp.concatenate([side(xw, slot * count, count) for _, slot in pairs], axis=1)
            parts = []
            for k in range(2):
                tall = jnp.concatenate([weights(high, k, m, g) for g, _ in pairs], axis=0)
                part = lax.dot_general(wide, tall, NN, preferred_element_type=F32)
                part = part[:2 * srcs], part[2 * srcs:]
                for g, slot in pairs:
                    small = lax.dot_general(
                        side(x8, slot * count, count), weights(low, k, m, g), NN,
                        preferred_element_type=F32,
                    )
                    part = part[0], part[1] + small * inv[slot][:, :1]
                parts.append(part[0] + part[1])
            trace[m, 0] += parts[0][:srcs] - parts[1][srcs:]
            trace[m, 1] += parts[1][:srcs] + parts[0][srcs:]

        last = min(LAST, groups)
        early = groups - last

        def ready(g, slot):
            arrived(g)
            prepare(incoming, [(zz, g) for zz in range(nop)], slot, xw, x8, slot * count)

        for n in range(3):
            for j in range(1, nop):
                fill(n, j).wait_recv()
        serve(c > served)
        take()

        @pl.loop(0, early)
        def _(g):
            ready(g, 0)
            for m in range(groups):
                multiply(m, [(g, 0)])

        for n in range(last):
            ready(early + n, n)

        @pl.loop(0, groups)
        def _(m):
            multiply(m, [(early + n, n) for n in range(last)])
            publish(m)

        serve(c < served)

    @pl.when(first)
    def _():
        pl.run_scoped(
            stream,
            pltpu.VMEM((STREAM_SLOTS, 2, group_rows, rows), F32),
            pltpu.VMEM((width // LANES, 4 * srcs, LANES), BF16),
            pltpu.VMEM((width // LANES, 2 * srcs, LANES), F8),
        )

    @pl.when(jnp.logical_not(first))
    def _():
        pl.run_scoped(
            resident,
            pltpu.VMEM((LOAD_SLOTS, LANES, piece), F32),
            pltpu.VMEM((2, blocks, width, LANES), BF16),
            pltpu.VMEM((2, blocks, width, LANES), F8),
            pltpu.VMEM((min(LAST, groups) * nop * split, 4 * srcs, LANES), BF16),
            pltpu.VMEM((min(LAST, groups) * nop * split, 2 * srcs, LANES), F8),
        )

    for n in range(3):
        for j in range(1, nop):
            fill(n, j).wait_send()

    @pl.loop(0, groups)
    def _(g):
        @pl.when(has_right)
        def _():
            to_right(g, 0).wait_send()

            @pl.when(straight(g))
            def _():
                for j in range(1, nop):
                    to_right(g, j).wait_send()

        @pl.when(lower)
        def _():
            for j in range(nop):
                to_upper(g, j).wait_send()

        @pl.when(spreads(g))
        def _():
            for j in range(1, nop):
                along(g, j).wait_send()

        @pl.when(jnp.logical_and(relays, lax.rem(g, 2) == 0))
        def _():
            for j in range(nop):
                pass_on(g, j).wait_send()


def solution(mesh):
    ncol, nrow, nop = (mesh.shape[a] for a in ("sx", "sy", "op"))

    def shards(op_real, op_imag, coef_right, coef_upper, sources):
        rows, width = op_real.shape[2:]
        srcs = sources.shape[3]
        groups = rows // 256 if rows % 256 == 0 else rows // 128
        group_rows = rows // groups
        pieces = PIECES if width % (PIECES * LANES) == 0 else 1
        vmem = pl.BlockSpec(memory_space=pltpu.VMEM)
        hbm = pl.BlockSpec(memory_space=pl.ANY)
        dma = pltpu.SemaphoreType.DMA
        out = pl.pallas_call(
            functools.partial(kernel, ncol, nrow, nop, groups, pieces),
            out_shape=jax.ShapeDtypeStruct((2, srcs, rows), F32),
            in_specs=[hbm, hbm, vmem, vmem, vmem],
            out_specs=vmem,
            scratch_shapes=[
                pltpu.VMEM((nop, 2, srcs, rows), F32),
                pltpu.VMEM((nop, 2, rows), F32),
                pltpu.VMEM((nop, 2, rows), F32),
                pltpu.VMEM((nop, groups, 2, srcs, group_rows), F32),
                pltpu.VMEM((nop, groups, 2, srcs, group_rows), F32),
                pltpu.VMEM((groups, 2, srcs, group_rows), F32),
                pltpu.VMEM((max(LAST, nop), 2 * srcs, LANES), F32),
                dma((max(STREAM_SLOTS, LOAD_SLOTS), 2)),
                dma((3, nop)),
                dma((3, nop)),
                dma((groups, nop)),
                dma((groups, nop)),
                dma((groups, nop)),
                dma((groups, nop)),
                dma((groups, nop)),
                pltpu.VMEM((groups, 2, srcs, group_rows), F32),
                dma((groups,)),
            ],
            compiler_params=pltpu.CompilerParams(
                collective_id=0, has_side_effects=True, vmem_limit_bytes=67043328
            ),
        )(op_real[0, 0], op_imag[0, 0], coef_right[0, 0], coef_upper[0, 0], sources[0, 0])
        return out[None, None]

    return jax.shard_map(
        shards,
        mesh=mesh,
        in_specs=(
            P("sx", "sy", "op", None),
            P("sx", "sy", "op", None),
            P("sx", "sy", None, "op"),
            P("sx", "sy", None, "op"),
            P("sx", "sy", None, None, "op"),
        ),
        out_specs=P("sx", "sy", None, None, "op"),
        check_vma=False,
    )
```

```python
import functools

import jax
import jax.numpy as jnp
from jax import lax
from jax.experimental import pallas as pl
from jax.experimental.pallas import tpu as pltpu
from jax.sharding import PartitionSpec as P

MESH = pl.DeviceIdType.MESH
LANES = 128
STREAM_SLOTS = 8
LAST = 3
PIECES = 3
LOAD_SLOTS = 5
LOW_SCALE = 2.0**20
F8 = jnp.float8_e4m3fn
F32 = jnp.float32
BF16 = jnp.bfloat16
NN = (((1,), (0,)), ((), ()))
NT = (((1,), (1,)), ((), ()))


def kernel(
    ncol, nrow, nop, groups, pieces,
    real_hbm, imag_hbm, right_ref, upper_ref, src_ref, out_ref,
    src_all, right_all, upper_all, left_all, below_all, trace, inv,
    load_sem, isend, irecv, lsend, lrecv, usend, bsend, brecv, relay, rrecv,
):
    c = lax.axis_index("sx")
    r = lax.axis_index("sy")
    z = lax.axis_index("op")
    first = c + r == 0
    rows, width = real_hbm.shape
    srcs = src_ref.shape[1]
    group_rows = rows // groups
    split = group_rows // LANES
    piece = width // pieces
    blocks = rows // LANES
    ops = (real_hbm, imag_hbm)
    has_left, has_right = c > 0, c < ncol - 1
    has_below, has_above = r > 0, r < nrow - 1

    mate = 1 - r
    lower = r == 0

    def peer(j):
        return lax.rem(z + j, nop)

    def meet():
        barrier = pltpu.get_barrier_semaphore()

        def greet(cc, rr, zz):
            pl.semaphore_signal(barrier, inc=1, device_id=(cc, rr, zz), device_id_type=MESH)

        for j in range(nop):
            greet(c, mate, peer(j))
        for j in range(1, nop):
            greet(c, r, peer(j))
        for there, step in ((has_right, 1), (has_left, -1)):
            @pl.when(there)
            def _():
                for j in range(nop):
                    greet(c + step, r, peer(j))

        @pl.when(lends)
        def _():
            greet(served, mate, z)

        @pl.when(relays)
        def _():
            greet(served, mate, z)
            for j in range(nop):
                greet(served + 1, mate, peer(j))

        @pl.when(gets)
        def _():
            for j in range(nop):
                greet(lax.rem(c + 1, 4), mate, peer(j))

        near = jnp.where(has_left, nop, 0) + jnp.where(has_right, nop, 0)
        near += jnp.where(lends, 1, 0) + jnp.where(relays, nop + 1, 0) + jnp.where(gets, nop, 0)
        pl.semaphore_wait(barrier, 2 * nop - 1 + near)
        src_all[z] = src_ref[...]
        right_all[z] = right_ref[...]
        upper_all[z] = upper_ref[...]

    def spread():
        for n in (2, 0, 1):
            for j in range(1, nop):
                fill(n, j).start()

    def fill(n, j):
        mine, whole = ((right_ref, right_all), (upper_ref, upper_all), (src_ref, src_all))[n]
        return pltpu.make_async_remote_copy(
            mine, whole.at[z], isend.at[n, j], irecv.at[n, j],
            device_id=(c, r, peer(j)), device_id_type=MESH,
        )

    def to_right(g, j):
        return pltpu.make_async_remote_copy(
            trace.at[g], left_all.at[z, g], lsend.at[g, j], lrecv.at[g, j],
            device_id=(c + 1, r, peer(j)), device_id_type=MESH,
        )

    def to_upper(g, j):
        return pltpu.make_async_remote_copy(
            trace.at[g], below_all.at[z, g], usend.at[g, j], brecv.at[g, j],
            device_id=(c, mate, peer(j)), device_id_type=MESH,
        )

    detour = ncol == 4
    late = (groups - 1) // 2 * 2
    served = lax.rem(c + 2, 4)
    lends = jnp.logical_and(jnp.logical_and(lower, detour), jnp.logical_and(c > 0, has_right))
    relays = jnp.logical_and(
        jnp.logical_and(has_below, detour), jnp.logical_and(served > 0, served < ncol - 1)
    )
    gets = jnp.logical_and(jnp.logical_and(lower, detour), c > 1)

    def straight(g):
        return jnp.logical_or(has_below, jnp.logical_and(c == 0, g < late))

    def lent(g):
        return jnp.logical_and(lends, lax.rem(g, 2) == 0)

    def spreads(g):
        own = jnp.logical_or(c > 1, jnp.logical_and(c == 1, g >= late))
        direct = jnp.logical_and(gets, lax.rem(g, 2) == 0)
        return jnp.logical_and(jnp.logical_and(lower, own), jnp.logical_not(direct))

    def lend(g):
        return pltpu.make_async_remote_copy(
            trace.at[g], relay.at[g], lsend.at[g, 0], rrecv.at[g],
            device_id=(lax.rem(c + 2, 4), mate, z), device_id_type=MESH,
        )

    def pass_on(g, j):
        return pltpu.make_async_remote_copy(
            relay.at[g], left_all.at[z, g], bsend.at[g, j], lrecv.at[g, j],
            device_id=(served + 1, mate, peer(j)), device_id_type=MESH,
        )

    def serve(when):
        @pl.when(jnp.logical_and(relays, when))
        def _():
            @pl.loop(0, (groups + 1) // 2)
            def _(n):
                lend(2 * n).wait_recv()
                for j in range(nop):
                    pass_on(2 * n, j).start()

    def along(g, j):
        return pltpu.make_async_remote_copy(
            left_all.at[z, g], left_all.at[z, g], bsend.at[g, j], lrecv.at[g, j],
            device_id=(c, r, peer(j)), device_id_type=MESH,
        )

    def span(g):
        return pl.ds(pl.multiple_of(g * group_rows, LANES), group_rows)

    def publish(g):
        @pl.when(has_right)
        def _():
            @pl.when(lent(g))
            def _():
                lend(g).start()

            @pl.when(jnp.logical_not(lent(g)))
            def _():
                to_right(g, 0).start()

            @pl.when(straight(g))
            def _():
                for j in range(1, nop):
                    to_right(g, j).start()

        @pl.when(lower)
        def _():
            for j in range(nop):
                to_upper(g, j).start()

        out_ref[:, :, span(g)] = trace[g]

    def take():
        @pl.loop(0, groups)
        def _(g):
            @pl.when(spreads(g))
            def _():
                to_right(g, 0).wait_recv()
                for j in range(1, nop):
                    along(g, j).start()

    def arrived(g):
        @pl.when(has_left)
        def _():
            for j in range(1, nop):
                to_right(g, j).wait_recv()

            @pl.when(jnp.logical_not(spreads(g)))
            def _():
                to_right(g, 0).wait_recv()

        @pl.when(has_below)
        def _():
            for j in range(nop):
                to_upper(g, j).wait_recv()

    def source(zz, g, h):
        cols = pl.ds(pl.multiple_of(g * group_rows + h * LANES, LANES), LANES)
        return [src_all[zz, k, :, cols] for k in range(2)]

    def incoming(zz, g, h):
        cols = pl.ds(pl.multiple_of(g * group_rows + h * LANES, LANES), LANES)
        lanes = slice(h * LANES, (h + 1) * LANES)
        value = source(zz, g, h)
        for coef, field in ((right_all, left_all), (upper_all, below_all)):
            cr, ci = coef[zz, 0:1, cols], coef[zz, 1:2, cols]
            fr, fi = field[zz, g, 0, :, lanes], field[zz, g, 1, :, lanes]
            value = [value[0] + (cr * fr - ci * fi), value[1] + (cr * fi + ci * fr)]
        return value

    def prepare(get, steps, slot, xw, x8, base):
        pairs = [get(zz, g, h) for zz, g in steps for h in range(split)]
        most = None
        for pair in pairs:
            both = jnp.maximum(jnp.abs(pair[0]), jnp.abs(pair[1]))
            most = both if most is None else jnp.maximum(most, both)
        top = jnp.maximum(jnp.max(most, axis=1, keepdims=True), 1e-30)
        scale = 256.0 / top
        back = top * (1.0 / (256.0 * LOW_SCALE))
        inv[slot] = jnp.broadcast_to(jnp.concatenate([back, back], axis=0), (2 * srcs, LANES))
        for n, pair in enumerate(pairs):
            for k in range(2):
                top_part = pair[k].astype(BF16)
                xw[base + n, k * srcs:(k + 1) * srcs, :] = top_part
                xw[base + n, (2 + k) * srcs:(3 + k) * srcs, :] = (
                    pair[k] - top_part.astype(F32)
                ).astype(BF16)
            x8[base + n] = jnp.concatenate([pair[0] * scale, pair[1] * scale], axis=0).astype(F8)

    def side(ref, base, count):
        return jnp.concatenate([ref[base + n] for n in range(count)], axis=1)

    def merge(big, small, slot):
        return big[:2 * srcs] + (big[2 * srcs:] + small * inv[slot][:, :1])

    def stream(stage, xw, x8):
        slots = stage.shape[0]
        seg = rows
        paired = groups // 2 * 2
        early = nop * paired
        half = nop // 2
        chunks = early + 2 * half * (groups - paired)

        def units(i):
            k = lax.rem(i, 2)
            a, b = i // 2, (i - early) // 2
            in_pairs = i < early
            first_m = jnp.where(in_pairs, 2 * lax.rem(a, paired // 2), paired + b // half)
            first_j = jnp.where(in_pairs, a // (paired // 2), 2 * lax.rem(b, half))
            second_m = jnp.where(in_pairs, first_m + 1, first_m)
            second_j = jnp.where(in_pairs, first_j, first_j + 1)
            return k, ((first_m, first_j), (second_m, second_j))

        def hop(n):
            return n

        def owner(n):
            return lax.rem(z - hop(n) + nop, nop)

        def load(i, u, op_k):
            _, pair = units(i)
            m, j = pair[u]
            slot = lax.rem(i, slots)
            return pltpu.make_async_copy(
                ops[op_k].at[
                    pl.ds(pl.multiple_of(m * group_rows, LANES), group_rows),
                    pl.ds(pl.multiple_of(owner(j) * seg, LANES), seg),
                ],
                stage.at[slot, u], load_sem.at[slot, u],
            )

        def fetch(i, op_k):
            for u in range(2):
                load(i, u, op_k).start()

        for i in range(slots):
            fetch(i, i % 2)
        meet()
        spread()
        trace[...] = jnp.zeros_like(trace)

        def chunk(i, op_k):
            _, pair = units(i)
            slot = lax.rem(i, slots)
            for u in range(2):
                load(i, u, op_k).wait()
            for u in range(2):
                m, j = pair[u]
                base = owner(j) * (groups * split)
                value = stage[slot, u]
                top_part = value.astype(BF16)
                rest = ((value - top_part.astype(F32)) * LOW_SCALE).astype(F8)
                big = lax.dot_general(side(xw, base, groups * split), top_part, NT, preferred_element_type=F32)
                small = lax.dot_general(side(x8, base, groups * split), rest, NT, preferred_element_type=F32)
                part = merge(big, small, j)
                if op_k == 0:
                    trace[m, 0] += part[:srcs]
                    trace[m, 1] += part[srcs:]
                else:
                    trace[m, 0] -= part[srcs:]
                    trace[m, 1] += part[:srcs]

            @pl.when(i + slots < chunks)
            def _():
                fetch(i + slots, op_k)

        @pl.loop(0, nop)
        def _(j):
            @pl.when(j > 0)
            def _():
                for n in range(3):
                    fill(n, hop(j)).wait_recv()

            steps = [(owner(j), g) for g in range(groups)]
            prepare(source, steps, j, xw, x8, owner(j) * (groups * split))

            @pl.loop(0, paired // 2)
            def _(a):
                for op_k in range(2):
                    chunk(2 * (j * (paired // 2) + a) + op_k, op_k)

                @pl.when(j == nop - 1)
                def _():
                    publish(2 * a)
                    publish(2 * a + 1)

        @pl.loop(0, groups - paired)
        def _(n):
            @pl.loop(0, half)
            def _(b):
                for op_k in range(2):
                    chunk(early + 2 * (n * half + b) + op_k, op_k)

            publish(paired + n)

    def resident(stage, high, low, xw, x8):
        slots = stage.shape[0]
        per = 2 * pieces
        chunks = per * blocks

        def load(i, n):
            k, p = n // pieces, n % pieces
            at = pl.multiple_of((i // per) * LANES, LANES)
            slot = lax.rem(i, slots)
            return pltpu.make_async_copy(
                ops[k].at[pl.ds(at, LANES), pl.ds(p * piece, piece)],
                stage.at[slot], load_sem.at[slot, 0],
            )

        for i in range(slots):
            load(i, i % per).start()
        meet()

        @pl.when(lower)
        def _():
            spread()


        @pl.when(jnp.logical_not(has_left))
        def _():
            left_all[...] = jnp.zeros_like(left_all)

        @pl.when(jnp.logical_not(has_below))
        def _():
            below_all[...] = jnp.zeros_like(below_all)

        @pl.loop(0, blocks)
        def _(blk):
            @pl.when(jnp.logical_and(has_below, blk == jnp.where(c == 0, blocks // 3, blocks // 2 - 1)))
            def _():
                spread()

            for n in range(per):
                i = blk * per + n
                load(i, n).wait()
                value = stage[lax.rem(i, slots)].T
                top_part = value.astype(BF16)
                k, p = n // pieces, n % pieces
                cols = slice(p * piece, (p + 1) * piece)
                high[k, blk, cols, :] = top_part
                low[k, blk, cols, :] = ((value - top_part.astype(F32)) * LOW_SCALE).astype(F8)

                @pl.when(i + slots < chunks)
                def _():
                    load(i + slots, (n + slots) % per).start()

        trace[...] = jnp.zeros_like(trace)

        def weights(ref, k, m, g):
            tiles = []
            for zz in range(nop):
                at = pl.ds(pl.multiple_of(zz * rows + g * group_rows, LANES), group_rows)
                tiles.append(jnp.concatenate(
                    [ref[k, m * split + h, at, :] for h in range(split)], axis=1
                ))
            return jnp.concatenate(tiles, axis=0)

        count = nop * split

        def multiply(m, pairs):
            wide = jnp.concatenate([side(xw, slot * count, count) for _, slot in pairs], axis=1)
            parts = []
            for k in range(2):
                tall = jnp.concatenate([weights(high, k, m, g) for g, _ in pairs], axis=0)
                part = lax.dot_general(wide, tall, NN, preferred_element_type=F32)
                part = part[:2 * srcs], part[2 * srcs:]
                for g, slot in pairs:
                    small = lax.dot_general(
                        side(x8, slot * count, count), weights(low, k, m, g), NN,
                        preferred_element_type=F32,
                    )
                    part = part[0], part[1] + small * inv[slot][:, :1]
                parts.append(part[0] + part[1])
            trace[m, 0] += parts[0][:srcs] - parts[1][srcs:]
            trace[m, 1] += parts[1][:srcs] + parts[0][srcs:]

        last = min(LAST, groups)
        early = groups - last

        def ready(g, slot):
            arrived(g)
            prepare(incoming, [(zz, g) for zz in range(nop)], slot, xw, x8, slot * count)

        for n in range(3):
            for j in range(1, nop):
                fill(n, j).wait_recv()
        serve(c > served)
        take()

        @pl.loop(0, early)
        def _(g):
            ready(g, 0)
            for m in range(groups):
                multiply(m, [(g, 0)])

        for n in range(last):
            ready(early + n, n)

        @pl.loop(0, groups)
        def _(m):
            multiply(m, [(early + n, n) for n in range(last)])
            publish(m)

        serve(c < served)

    @pl.when(first)
    def _():
        pl.run_scoped(
            stream,
            pltpu.VMEM((STREAM_SLOTS, 2, group_rows, rows), F32),
            pltpu.VMEM((width // LANES, 4 * srcs, LANES), BF16),
            pltpu.VMEM((width // LANES, 2 * srcs, LANES), F8),
        )

    @pl.when(jnp.logical_not(first))
    def _():
        pl.run_scoped(
            resident,
            pltpu.VMEM((LOAD_SLOTS, LANES, piece), F32),
            pltpu.VMEM((2, blocks, width, LANES), BF16),
            pltpu.VMEM((2, blocks, width, LANES), F8),
            pltpu.VMEM((min(LAST, groups) * nop * split, 4 * srcs, LANES), BF16),
            pltpu.VMEM((min(LAST, groups) * nop * split, 2 * srcs, LANES), F8),
        )

    for n in range(3):
        for j in range(1, nop):
            fill(n, j).wait_send()

    @pl.loop(0, groups)
    def _(g):
        @pl.when(has_right)
        def _():
            to_right(g, 0).wait_send()

            @pl.when(straight(g))
            def _():
                for j in range(1, nop):
                    to_right(g, j).wait_send()

        @pl.when(lower)
        def _():
            for j in range(nop):
                to_upper(g, j).wait_send()

        @pl.when(spreads(g))
        def _():
            for j in range(1, nop):
                along(g, j).wait_send()

        @pl.when(jnp.logical_and(relays, lax.rem(g, 2) == 0))
        def _():
            for j in range(nop):
                pass_on(g, j).wait_send()


def solution(mesh):
    ncol, nrow, nop = (mesh.shape[a] for a in ("sx", "sy", "op"))

    def shards(op_real, op_imag, coef_right, coef_upper, sources):
        rows, width = op_real.shape[2:]
        srcs = sources.shape[3]
        groups = rows // 256 if rows % 256 == 0 else rows // 128
        group_rows = rows // groups
        pieces = PIECES if width % (PIECES * LANES) == 0 else 1
        vmem = pl.BlockSpec(memory_space=pltpu.VMEM)
        hbm = pl.BlockSpec(memory_space=pl.ANY)
        dma = pltpu.SemaphoreType.DMA
        out = pl.pallas_call(
            functools.partial(kernel, ncol, nrow, nop, groups, pieces),
            out_shape=jax.ShapeDtypeStruct((2, srcs, rows), F32),
            in_specs=[hbm, hbm, vmem, vmem, vmem],
            out_specs=vmem,
            scratch_shapes=[
                pltpu.VMEM((nop, 2, srcs, rows), F32),
                pltpu.VMEM((nop, 2, rows), F32),
                pltpu.VMEM((nop, 2, rows), F32),
                pltpu.VMEM((nop, groups, 2, srcs, group_rows), F32),
                pltpu.VMEM((nop, groups, 2, srcs, group_rows), F32),
                pltpu.VMEM((groups, 2, srcs, group_rows), F32),
                pltpu.VMEM((max(LAST, nop), 2 * srcs, LANES), F32),
                dma((max(STREAM_SLOTS, LOAD_SLOTS), 2)),
                dma((3, nop)),
                dma((3, nop)),
                dma((groups, nop)),
                dma((groups, nop)),
                dma((groups, nop)),
                dma((groups, nop)),
                dma((groups, nop)),
                pltpu.VMEM((groups, 2, srcs, group_rows), F32),
                dma((groups,)),
            ],
            compiler_params=pltpu.CompilerParams(
                collective_id=0, has_side_effects=True, vmem_limit_bytes=67043328
            ),
        )(op_real[0, 0], op_imag[0, 0], coef_right[0, 0], coef_upper[0, 0], sources[0, 0])
        return out[None, None]

    return jax.shard_map(
        shards,
        mesh=mesh,
        in_specs=(
            P("sx", "sy", "op", None),
            P("sx", "sy", "op", None),
            P("sx", "sy", None, "op"),
            P("sx", "sy", None, "op"),
            P("sx", "sy", None, None, "op"),
        ),
        out_specs=P("sx", "sy", None, None, "op"),
        check_vma=False,
    )
```
